32 devices in a mesh: feat: 16 (over z, x, core), samp: 2 (over y).
Axes of the slice: x: 2, y: 2, z: 4, core: 2. Of those that a mesh axis runs over, the one named last changes fastest.
Arguments:
- features: bfloat16 [4096, 16384], P('samp', 'feat'), may hold values from -0.046875 to 0.046875
- labels: int32 [4096], P('samp'), may hold values 0 or 1
- weights: float32 [16384], P('feat'), may hold values from -6 to 6
- sampled: int32 [2048], P('samp'), may hold values from 0 to 2047
Outputs:
- step: float32 [16384], P('feat')
The draws below stay inside these ranges and needn't reach their ends.
Inputs may be any that keep to these rules, and one draw needn't show every extreme that they name: `sampled`: entries i * 1024 to (i + 1) * 1024 - 1 name rows of the i-th block of 2048 data rows, counted from that block's start; rows may repeat.
All inputs are finite; a program needn't handle non-finite values. No bound on the sum of `labels` on one device may be relied on, other than what follows from the above.
Results may differ from the reference program's by a relative error of at most 0.0025.
Values may be sent and summed in bfloat16 or wider, within the bound.
A program may use at most 64 MiB of HBM per device.

```python
import jax
import jax.numpy as jnp
from jax import lax

F = 16384
BLK = 512
R_DEV = 2048
HS_DEV = 1024
ITERS = 3
ROWS = 4096
HS_TOTAL = 2048
N_SAMP = 2


def set_ends(values, own_key, low, high):
    place = [jax.random.randint(jax.random.fold_in(own_key, axis), (), 0, length) for axis, length in enumerate(values.shape)]
    main_axis = values.shape.index(max(values.shape))
    next_to = place[:main_axis] + [(place[main_axis] + 1) % values.shape[main_axis]] + place[main_axis + 1:]
    return values.at[tuple(place)].set(low).at[tuple(next_to)].set(high)


def block_scale(rng, shape, split, smallest, high):
    level = 1.0
    for dim, blocks in split:
        steps = jax.random.uniform(jax.random.fold_in(jax.random.fold_in(rng, 6), dim), (blocks,), jnp.float32, smallest / len(split), high / len(split))
        level = level * jnp.repeat(jnp.exp(steps), shape[dim] // blocks).reshape((-1,) + (1,) * (len(shape) - 1 - dim))
    return level


def centred(stream_key, shape, width, reach, cuts=(), kind=jnp.bfloat16):
    result = width * jax.random.normal(stream_key, shape, jnp.float32)
    if cuts:
        result = result * block_scale(stream_key, shape, cuts, -0.22, 0.18)
    return jnp.clip(result, -reach, reach).astype(kind)


def setup_inputs(seed: int = 0) -> dict:
    arg_keys = jax.random.split(jax.random.key(seed), 5)
    return {
        "features": centred(arg_keys[0], (ROWS, F), (F ** -0.5), 0.046875, ((0, 2), (1, 16))),
        "labels": set_ends((jax.random.randint(arg_keys[1], (ROWS,), 0, 2) < 1).astype(jnp.int32), jax.random.fold_in(arg_keys[1], 1), 0, 1),
        "weights": centred(arg_keys[2], (F,), 1.0, 6.0, ((0, 16),), jnp.float32),
        "sampled": set_ends(jax.random.randint(arg_keys[3], (HS_TOTAL,), 0, R_DEV), jax.random.fold_in(arg_keys[3], 1), 0, R_DEV - 1).astype(jnp.int32),
    }


RIDGE_COEF = 0.05

def exact_dot(left, right):
    return jnp.dot(left.astype(jnp.float32), right.astype(jnp.float32), precision=lax.Precision.HIGHEST, preferred_element_type=jnp.float32)

def block_solve(factors, rhs_blocks):
    forward = jax.vmap(lambda factor, column: jax.scipy.linalg.solve_triangular(factor, column, lower=True))(factors, rhs_blocks)
    return jax.vmap(lambda factor, column: jax.scipy.linalg.solve_triangular(factor, column, lower=True, trans=1))(factors, forward)

def reference(features, labels, weights, sampled):
    count = F // BLK
    ridge_term = RIDGE_COEF / F
    row_total = R_DEV * N_SAMP
    hess_total = HS_DEV * N_SAMP
    block_ids = jnp.arange(count, dtype=jnp.int32)
    weight_blocks = weights.reshape(count, BLK)

    def column_block(index):
        return lax.dynamic_slice_in_dim(features, (index * BLK).astype(jnp.int32), BLK, 1)
    margin = lax.optimization_barrier(jnp.sum(lax.map(lambda index: exact_dot(column_block(index).astype(jnp.float32), weight_blocks[index]), block_ids), axis=0))
    probability = jax.nn.sigmoid(margin)
    residue = probability - labels.astype(jnp.float32)
    grad_blocks = lax.map(lambda index: exact_dot(residue, column_block(index).astype(jnp.float32)), block_ids)
    gradient = grad_blocks.reshape(F) / row_total + ridge_term * weights
    global_rows = (sampled + jnp.arange(hess_total, dtype=jnp.int32) // HS_DEV * R_DEV).astype(jnp.int32)
    chosen = probability[global_rows]
    root_curv = jnp.sqrt(chosen * (1.0 - chosen))

    def scaled_block(index):
        return (jnp.take(column_block(index), global_rows, axis=0) * root_curv[:, None]).astype(jnp.bfloat16)
    scaled = lax.map(scaled_block, block_ids)

    def gram_block(block):
        wide = block.astype(jnp.float32)
        return exact_dot(wide.T, wide)
    gram = lax.map(gram_block, scaled) / hess_total + ridge_term * jnp.eye(BLK, dtype=jnp.float32)
    factors = jnp.linalg.cholesky(gram)

    def precondition(vector):
        return block_solve(factors, vector.reshape(count, BLK)).reshape(F)

    def curvature(vector):
        pieces = lax.map(lambda items: exact_dot(items[0].astype(jnp.float32), items[1]), (scaled, vector.reshape(count, BLK)))
        image_rows = lax.optimization_barrier(jnp.sum(pieces, axis=0))
        back = lax.map(lambda block: exact_dot(image_rows, block.astype(jnp.float32)), scaled).reshape(F)
        return back / hess_total + ridge_term * vector
    solution = jnp.zeros((F,), jnp.float32)
    residual = -gradient
    precond = precondition(residual)
    direction = precond
    rz_now = jnp.sum(residual * precond)
    for iteration in range(ITERS):
        image = curvature(direction)
        alpha = rz_now / jnp.sum(direction * image)
        solution = solution + alpha * direction
        residual = residual - alpha * image
        if iteration + 1 < ITERS:
            precond = precondition(residual)
            fresh = jnp.sum(residual * precond)
            direction = precond + fresh / rz_now * direction
            rz_now = fresh
    return solution
```

```python
import functools

import jax
import jax.numpy as jnp
from jax import lax
from jax.experimental import pallas as pl
from jax.experimental.pallas import tpu as pltpu
from jax.sharding import PartitionSpec as P

F = 16384
BLK = 512
ITERS = 3
QUAD = 4
MESH = pl.DeviceIdType.MESH


RIDGE_COEF = 0.05


def partner_2(value, axis, apart):
    mask = 2**apart
    pairs = [(source, source ^ mask) for source in range(lax.axis_size(axis))]
    return lax.ppermute(value, axis, pairs)


def split_parts(vector):
    upper_part = vector.astype(jnp.bfloat16)
    widened = lax.optimization_barrier(upper_part).astype(jnp.float32)
    lower_part = (vector - widened).astype(jnp.bfloat16)
    return (upper_part, lower_part)


def matrix_vector(matrix, vector):
    upper_part, lower_part = split_parts(vector)
    return jnp.dot(matrix, upper_part, preferred_element_type=jnp.float32) + jnp.dot(
        matrix, lower_part, preferred_element_type=jnp.float32
    )


def vector_matrix(vector, matrix):
    upper_part, lower_part = split_parts(vector)
    return jnp.dot(upper_part, matrix, preferred_element_type=jnp.float32) + jnp.dot(
        lower_part, matrix, preferred_element_type=jnp.float32
    )


def block_solve(factors, rhs_blocks):
    forward = jax.vmap(
        lambda factor, column: jax.scipy.linalg.solve_triangular(factor, column, lower=True)
    )(factors, rhs_blocks)
    return jax.vmap(
        lambda factor, column: jax.scipy.linalg.solve_triangular(
            factor, column, lower=True, trans=1
        )
    )(factors, forward)


def local_blocks(scaled):
    blocks = scaled.reshape(scaled.shape[0], scaled.shape[1] // BLK, BLK)
    return jnp.einsum("hkb,hkc->kbc", blocks, blocks, preferred_element_type=jnp.float32)


def per_device(features, labels, weights, sampled):
    columns = features.shape[1]
    sample_rows = sampled.shape[0]
    groups = lax.axis_size("samp")
    row_total = features.shape[0] * groups
    hess_total = sample_rows * groups
    ridge_term = RIDGE_COEF / F
    paired = columns < BLK
    upper_side = lax.axis_index("feat") % 2 == 1
    margin = lax.psum(matrix_vector(features, weights), "feat")
    probability = jax.nn.sigmoid(margin)
    residue = probability - labels.astype(jnp.float32)
    gradient = lax.psum(vector_matrix(residue, features), "samp") / row_total + ridge_term * weights
    chosen = jnp.take(probability, sampled)
    root_curv = jnp.sqrt(chosen * (1.0 - chosen))
    scaled = (jnp.take(features, sampled, axis=0) * root_curv[:, None]).astype(jnp.bfloat16)
    if paired:
        partner = partner_2(scaled, "feat", 0)
        joined = jnp.where(
            upper_side, jnp.concatenate([partner, scaled], 1), jnp.concatenate([scaled, partner], 1)
        )
        partial_gram = jnp.einsum("hb,hc->bc", joined, joined, preferred_element_type=jnp.float32)[
            None
        ]
    else:
        partial_gram = local_blocks(scaled)
    summed = lax.psum(partial_gram, "samp")
    gram = summed / hess_total + ridge_term * jnp.eye(BLK, dtype=jnp.float32)
    factors = jnp.linalg.cholesky(gram)

    def precondition(vector):
        if paired:
            other = partner_2(vector, "feat", 0)
            joined_vec = jnp.where(
                upper_side, jnp.concatenate([other, vector]), jnp.concatenate([vector, other])
            )[None]
            solved = block_solve(factors, joined_vec)[0]
            return jnp.where(upper_side, solved[columns:], solved[:columns])
        return block_solve(factors, vector.reshape(-1, BLK)).reshape(columns)

    def curvature(vector):
        image_rows = lax.psum(matrix_vector(scaled, vector), "feat")
        back = lax.psum(vector_matrix(image_rows, scaled), "samp")
        return back / hess_total + ridge_term * vector

    solution = jnp.zeros((columns,), jnp.float32)
    residual = -gradient

    def both_dots(resid_vec, precond_vec, image_vec):
        return lax.psum(
            (jnp.sum(resid_vec * precond_vec), jnp.sum(image_vec * precond_vec)), "feat"
        )

    precond = precondition(residual)
    image = curvature(precond)
    rz_now, wz_now = both_dots(residual, precond, image)
    alpha = rz_now / wz_now
    direction = precond
    along = image
    for iteration in range(ITERS):
        solution = solution + alpha * direction
        residual = residual - alpha * along
        if iteration + 1 < ITERS:
            precond = precondition(residual)
            image = curvature(precond)
            fresh, wz_now = both_dots(residual, precond, image)
            beta = fresh / rz_now
            alpha = fresh / (wz_now - beta * fresh / alpha)
            direction = precond + beta * direction
            along = image + beta * along
            rz_now = fresh
    return solution

def split_rows(row):
    top = row.astype(jnp.bfloat16).astype(jnp.float32)
    rest = row - top
    middle = rest.astype(jnp.bfloat16).astype(jnp.float32)
    bottom = rest - middle
    shape = (16, row.shape[1])
    line = lax.broadcasted_iota(jnp.int32, shape, 0)
    spread = lambda part: jnp.broadcast_to(part, shape)
    picked = jnp.where(
        line == 0,
        spread(top),
        jnp.where(line == 1, spread(middle), jnp.where(line == 2, spread(bottom), 0.0)),
    )
    return picked.astype(jnp.bfloat16)


def add_rows(parts):
    return parts[0:1] + parts[1:2] + parts[2:3]


def mxu(left, right, left_dim, right_dim):
    return lax.dot_general(
        left, right, (((left_dim,), (right_dim,)), ((), ())), preferred_element_type=jnp.float32
    )


def row_times(row, matrix):
    return add_rows(mxu(split_rows(row), matrix, 1, 0))


def row_times_transposed(row, matrix):
    return add_rows(mxu(split_rows(row), matrix, 1, 1))


def place():
    feat = lax.axis_index("feat")
    samp = lax.axis_index("samp")
    return feat // QUAD, feat % QUAD, samp


def greet(peers):
    barrier = pltpu.get_barrier_semaphore()
    for peer in peers:
        pl.semaphore_signal(barrier, inc=1, device_id=peer, device_id_type=MESH)
    return lambda: pl.semaphore_wait(barrier, len(peers))


def remote(source, target, send_sem, recv_sem, peer):
    return pltpu.make_async_remote_copy(
        src_ref=source,
        dst_ref=target,
        send_sem=send_sem,
        recv_sem=recv_sem,
        device_id=peer,
        device_id_type=MESH,
    )


def start_exchange(slots, mine, peers, send_sems, recv_sems):
    copies = []
    for number, peer in enumerate(peers):
        copy = remote(
            slots.at[mine], slots.at[mine], send_sems.at[number], recv_sems.at[number], peer
        )
        copy.start()
        copies.append(copy)
    return copies


def finish(copies):
    for copy in copies:
        copy.wait()


def total_of(slots, count):
    value = slots[0]
    for number in range(1, count):
        value = value + slots[number]
    return value


def quad_peers(depth, quarter, samp):
    return [{"feat": depth * QUAD + (quarter + k) % QUAD, "samp": samp} for k in range(1, QUAD)]


def depth_peers(layers, depth, quarter, samp):
    return [
        {"feat": ((depth + k) % layers) * QUAD + quarter, "samp": samp} for k in range(1, layers)
    ]


def plane_peers(depth, quarter, samp):
    member = samp * QUAD + quarter
    peers = []
    for k in range(1, 2 * QUAD):
        other = (member + k) % (2 * QUAD)
        peers.append({"feat": depth * QUAD + other % QUAD, "samp": other // QUAD})
    return peers


CHUNKS = 4


def gram_kernel(
    layers, features, weights, labels, sampled,
    scaled, gram, gradient,
    chosen, own_rows, sent_rows, came_rows, quad_slots, depth_slots, root_sent, root_came, grad_sent, grad_came,
    ship_send, ship_recv, quad_send, quad_recv, depth_send, depth_recv, small_send, small_recv,
):
    depth, quarter, samp = place()
    rows, columns = features.shape
    samples = sampled.shape[0]
    half = columns // 2
    partner = {"feat": depth * QUAD + quarter, "samp": 1 - samp}
    across = quad_peers(depth, quarter, samp)
    along = depth_peers(layers, depth, quarter, samp)
    wait_all = greet([partner] + across + along)
    mine_at = pl.multiple_of(samp * half, 128)
    other_at = pl.multiple_of((1 - samp) * half, 128)
    piece = samples // CHUNKS

    quad_slots[quarter] = row_times_transposed(weights[...], features[...])
    wait_all()
    quad_copies = start_exchange(quad_slots, quarter, across, quad_send, quad_recv)

    def ship(number):
        first = number * piece
        return remote(
            sent_rows.at[pl.ds(first, piece)],
            came_rows.at[pl.ds(first, piece)],
            ship_send.at[number],
            ship_recv.at[number],
            partner,
        )

    def pick(number, carry):
        first = pl.multiple_of(number * piece, 128)
        names = jnp.broadcast_to(sampled[pl.ds(first, piece), :], (piece, rows))
        hot = jnp.where(lax.broadcasted_iota(jnp.int32, (piece, rows), 1) == names, 1.0, 0.0)
        hot = hot.astype(jnp.bfloat16)
        chosen[pl.ds(first, piece), :] = hot
        sent_rows[pl.ds(first, piece), :] = mxu(hot, features[:, pl.ds(other_at, half)], 1, 0).astype(
            jnp.bfloat16
        )
        ship(number).start()
        return carry

    lax.fori_loop(0, CHUNKS, pick, 0)
    finish(quad_copies)
    depth_slots[depth] = total_of(quad_slots, QUAD)
    depth_copies = start_exchange(depth_slots, depth, along, depth_send, depth_recv)

    def pick_own(number, carry):
        first = pl.multiple_of(number * piece, 128)
        own_rows[pl.ds(first, piece), :] = mxu(
            chosen[pl.ds(first, piece), :], features[:, pl.ds(mine_at, half)], 1, 0
        ).astype(jnp.bfloat16)
        return carry

    lax.fori_loop(0, CHUNKS, pick_own, 0)
    finish(depth_copies)
    margin = total_of(depth_slots, layers)
    probability = 1.0 / (1.0 + jnp.exp(-margin))
    root = jnp.sqrt(probability * (1.0 - probability))
    own_root = row_times_transposed(root, chosen[...])
    root_sent[...] = own_root
    root_copy = remote(root_sent, root_came, small_send.at[0], small_recv.at[0], partner)
    root_copy.start()
    residue = probability - labels[...].astype(jnp.float32)
    grad_sent[...] = row_times(residue, features[:, pl.ds(other_at, half)])
    grad_copy = remote(grad_sent, grad_came, small_send.at[1], small_recv.at[1], partner)
    grad_copy.start()
    own_grad = row_times(residue, features[:, pl.ds(mine_at, half)])

    def scale_into(source, root_row, start):
        factor = jnp.transpose(jnp.broadcast_to(root_row, (128, samples)))
        for column in range(0, half, 128):
            wide = source[:, column : column + 128].astype(jnp.float32) * factor
            scaled[pl.ds(start, samples), column : column + 128] = wide.astype(jnp.bfloat16)

    mine_row = pl.multiple_of(samp * samples, 128)
    other_row = pl.multiple_of((1 - samp) * samples, 128)
    scale_into(own_rows, own_root, mine_row)
    own_block = scaled[pl.ds(mine_row, samples), :]
    gram[...] = mxu(own_block, own_block, 0, 0)

    def settle(number, carry):
        ship(number).wait()
        return carry

    root_copy.wait()
    grad_copy.wait()
    ridge_term = RIDGE_COEF / F
    gradient[...] = (own_grad + grad_came[...]) / (2 * rows) + ridge_term * weights[
        :, pl.ds(mine_at, half)
    ]
    lax.fori_loop(0, CHUNKS, settle, 0)
    scale_into(came_rows, root_came[...], other_row)
    other_block = scaled[pl.ds(other_row, samples), :]
    both = gram[...] + mxu(other_block, other_block, 0, 0)
    diagonal = lax.broadcasted_iota(jnp.int32, both.shape, 0) == lax.broadcasted_iota(
        jnp.int32, both.shape, 1
    )
    gram[...] = both / (2 * samples) + jnp.where(diagonal, ridge_term, 0.0)


SQUARINGS = 8
POLISH = 2
LIMIT = 60


def halves(value):
    top = value.astype(jnp.bfloat16)
    return top, (value - top.astype(jnp.float32)).astype(jnp.bfloat16)


def inverse_kernel(gram, upper, lower, unit, inverse):
    order = gram.shape[0]
    bound = jnp.max(jnp.sum(jnp.abs(gram[...]), axis=0, keepdims=True))
    shape = (order, order)
    eye = jnp.where(
        lax.broadcasted_iota(jnp.int32, shape, 0) == lax.broadcasted_iota(jnp.int32, shape, 1),
        1.0,
        0.0,
    )
    normed = gram[...] / bound
    unit[...] = normed
    power = eye - normed
    inverse[...] = eye + power

    def square(_, power_now):
        squared = mxu(power_now, power_now, 1, 0)
        power_next = squared.astype(jnp.bfloat16)
        value = inverse[...]
        inverse[...] = value + mxu(value.astype(jnp.bfloat16), power_next, 1, 0)
        return power_next

    lax.fori_loop(0, SQUARINGS, square, power.astype(jnp.bfloat16))
    unit_top, unit_low = halves(unit[...])

    def polish(_, size):
        value = inverse[...]
        top, low = halves(value)
        product = mxu(unit_top, top, 1, 0) + mxu(unit_top, low, 1, 0) + mxu(unit_low, top, 1, 0)
        left = eye - product
        inverse[...] = value + mxu(top, left.astype(jnp.bfloat16), 1, 0)
        return jnp.sum(left * left)

    size = lax.fori_loop(0, POLISH, polish, jnp.float32(0.0))
    settled = size < 0.0025

    @pl.when(jnp.logical_not(settled))
    def _():
        inverse[...] = eye

        def exact(left, right):
            return jnp.dot(
                left, right, precision=lax.Precision.HIGHEST, preferred_element_type=jnp.float32
            )

        def going(state):
            count, size_now = state
            return jnp.logical_and(count < LIMIT, size_now > 1e-8)

        def step(state):
            count, _ = state
            value = inverse[...]
            left = eye - exact(unit[...], value)
            fresh = value + exact(value, left)
            inverse[...] = 0.5 * (fresh + jnp.transpose(fresh))
            return count + 1, jnp.sum(left * left)

        lax.while_loop(going, step, (jnp.int32(0), jnp.float32(1.0)))

    top, low = halves(inverse[...] / bound)
    upper[...] = top
    lower[...] = low


def descent_kernel(
    layers, scaled, upper, lower, gradient,
    step,
    plane_slots, depth_slots, last_sent, last_came,
    plane_send, plane_recv, depth_send, depth_recv, last_send, last_recv,
):
    depth, quarter, samp = place()
    samples, half = scaled.shape
    partner = {"feat": depth * QUAD + quarter, "samp": 1 - samp}
    plane = plane_peers(depth, quarter, samp)
    along = depth_peers(layers, depth, quarter, samp)
    wait_all = greet(plane + along)
    member = samp * QUAD + quarter
    ridge_term = RIDGE_COEF / F
    lane = lax.broadcasted_iota(jnp.int32, (1, 128), 1)

    def precondition(vector):
        parts = split_rows(vector)
        return add_rows(mxu(parts, upper[...], 1, 0) + mxu(parts, lower[...], 1, 0))

    def total(row):
        return jnp.sum(row, axis=1, keepdims=True)

    residual = -gradient[...]
    answer = jnp.zeros_like(residual)
    direction = jnp.zeros_like(residual)
    along_rows = None
    rz_now = None
    length = None
    for iteration in range(ITERS):
        precond = precondition(residual)
        numbers = jnp.where(
            lane == 0,
            total(residual * precond),
            jnp.where(
                lane == 1,
                total(precond * precond),
                jnp.where(lane == 2, total(precond * direction), 0.0),
            ),
        )
        mine = plane_slots.at[iteration, member]
        mine[:, :samples] = row_times_transposed(precond, scaled[...])
        mine[:, samples:] = numbers
        if iteration == 0:
            wait_all()
        finish(
            start_exchange(
                plane_slots.at[iteration], member, plane, plane_send.at[iteration], plane_recv.at[iteration]
            )
        )
        depth_slots[iteration, depth] = total_of(plane_slots.at[iteration], 2 * QUAD)
        finish(
            start_exchange(
                depth_slots.at[iteration], depth, along, depth_send.at[iteration], depth_recv.at[iteration]
            )
        )
        summed = total_of(depth_slots.at[iteration], layers)
        image_rows = summed[:, :samples]
        fresh = summed[:, samples : samples + 1]
        square = summed[:, samples + 1 : samples + 2]
        cross = summed[:, samples + 2 : samples + 3]
        if iteration == 0:
            direction = precond
            along_rows = image_rows
            length = square
        else:
            beta = fresh / rz_now
            direction = precond + beta * direction
            along_rows = image_rows + beta * along_rows
            length = square + 2.0 * beta * cross + beta * beta * length
        rz_now = fresh
        alpha = rz_now / (total(along_rows * along_rows) / samples + ridge_term * length)
        answer = answer + alpha * direction
        if iteration + 1 < ITERS:
            image = row_times(along_rows, scaled[...]) / samples + ridge_term * direction
            residual = residual - alpha * image
    last_sent[...] = answer
    final = remote(last_sent, last_came, last_send.at[0], last_recv.at[0], partner)
    final.start()
    step[:, pl.ds(pl.multiple_of(samp * half, 128), half)] = answer
    final.wait()
    step[:, pl.ds(pl.multiple_of((1 - samp) * half, 128), half)] = last_came[...]


def split_device(features, labels, weights, sampled):
    rows, columns = features.shape
    samples = sampled.shape[0]
    half = columns // 2
    layers = lax.axis_size("feat") // QUAD
    shaped = jax.ShapeDtypeStruct
    whole = pl.BlockSpec(memory_space=pltpu.VMEM)
    dma = pltpu.SemaphoreType.DMA
    vmem = pltpu.VMEM
    scaled, gram, gradient = pl.pallas_call(
        functools.partial(gram_kernel, layers),
        out_shape=(
            shaped((2 * samples, half), jnp.bfloat16),
            shaped((half, half), jnp.float32),
            shaped((1, half), jnp.float32),
        ),
        in_specs=[whole] * 4,
        out_specs=(whole,) * 3,
        scratch_shapes=[
            vmem((samples, rows), jnp.bfloat16),
            vmem((samples, half), jnp.bfloat16),
            vmem((samples, half), jnp.bfloat16),
            vmem((samples, half), jnp.bfloat16),
            vmem((QUAD, 1, rows), jnp.float32),
            vmem((layers, 1, rows), jnp.float32),
            vmem((1, samples), jnp.float32),
            vmem((1, samples), jnp.float32),
            vmem((1, half), jnp.float32),
            vmem((1, half), jnp.float32),
            dma((CHUNKS,)),
            dma((CHUNKS,)),
            dma((QUAD - 1,)),
            dma((QUAD - 1,)),
            dma((layers - 1,)),
            dma((layers - 1,)),
            dma((2,)),
            dma((2,)),
        ],
        compiler_params=pltpu.CompilerParams(collective_id=0, has_side_effects=True),
    )(features, weights[None, :], labels[None, :], sampled[:, None])
    upper, lower = pl.pallas_call(
        inverse_kernel,
        out_shape=(shaped((half, half), jnp.bfloat16),) * 2,
        in_specs=[whole],
        out_specs=(whole,) * 2,
        scratch_shapes=[vmem((half, half), jnp.float32), vmem((half, half), jnp.float32)],
    )(gram)
    width = 2 * samples + 128
    step = pl.pallas_call(
        functools.partial(descent_kernel, layers),
        out_shape=shaped((1, columns), jnp.float32),
        in_specs=[whole] * 4,
        out_specs=whole,
        scratch_shapes=[
            vmem((ITERS, 2 * QUAD, 1, width), jnp.float32),
            vmem((ITERS, layers, 1, width), jnp.float32),
            vmem((1, half), jnp.float32),
            vmem((1, half), jnp.float32),
            dma((ITERS, 2 * QUAD - 1)),
            dma((ITERS, 2 * QUAD - 1)),
            dma((ITERS, layers - 1)),
            dma((ITERS, layers - 1)),
            dma((1,)),
            dma((1,)),
        ],
        compiler_params=pltpu.CompilerParams(collective_id=1, has_side_effects=True),
    )(scaled, upper, lower, gradient)
    return step[0]


def solution(mesh):
    placed = (P("samp", "feat"), P("samp"), P("feat"), P("samp"))
    devices, groups = mesh.shape["feat"], mesh.shape["samp"]
    apart = groups == 2 and devices % QUAD == 0 and devices > QUAD and F // devices == 2 * BLK
    return jax.shard_map(
        split_device if apart else per_device,
        mesh=mesh,
        in_specs=placed,
        out_specs=P("feat"),
        check_vma=False,
    )
```

```python
import functools

import jax
import jax.numpy as jnp
from jax import lax
from jax.experimental import pallas as pl
from jax.experimental.pallas import tpu as pltpu
from jax.sharding import PartitionSpec as P

F = 16384
BLK = 512
ITERS = 3
QUAD = 4
MESH = pl.DeviceIdType.MESH


RIDGE_COEF = 0.05


def partner_2(value, axis, apart):
    mask = 2**apart
    pairs = [(source, source ^ mask) for source in range(lax.axis_size(axis))]
    return lax.ppermute(value, axis, pairs)


def split_parts(vector):
    upper_part = vector.astype(jnp.bfloat16)
    widened = lax.optimization_barrier(upper_part).astype(jnp.float32)
    lower_part = (vector - widened).astype(jnp.bfloat16)
    return (upper_part, lower_part)


def matrix_vector(matrix, vector):
    upper_part, lower_part = split_parts(vector)
    return jnp.dot(matrix, upper_part, preferred_element_type=jnp.float32) + jnp.dot(
        matrix, lower_part, preferred_element_type=jnp.float32
    )


def vector_matrix(vector, matrix):
    upper_part, lower_part = split_parts(vector)
    return jnp.dot(upper_part, matrix, preferred_element_type=jnp.float32) + jnp.dot(
        lower_part, matrix, preferred_element_type=jnp.float32
    )


def block_solve(factors, rhs_blocks):
    forward = jax.vmap(
        lambda factor, column: jax.scipy.linalg.solve_triangular(factor, column, lower=True)
    )(factors, rhs_blocks)
    return jax.vmap(
        lambda factor, column: jax.scipy.linalg.solve_triangular(
            factor, column, lower=True, trans=1
        )
    )(factors, forward)


def local_blocks(scaled):
    blocks = scaled.reshape(scaled.shape[0], scaled.shape[1] // BLK, BLK)
    return jnp.einsum("hkb,hkc->kbc", blocks, blocks, preferred_element_type=jnp.float32)


def per_device(features, labels, weights, sampled):
    columns = features.shape[1]
    sample_rows = sampled.shape[0]
    groups = lax.axis_size("samp")
    row_total = features.shape[0] * groups
    hess_total = sample_rows * groups
    ridge_term = RIDGE_COEF / F
    paired = columns < BLK
    upper_side = lax.axis_index("feat") % 2 == 1
    margin = lax.psum(matrix_vector(features, weights), "feat")
    probability = jax.nn.sigmoid(margin)
    residue = probability - labels.astype(jnp.float32)
    gradient = lax.psum(vector_matrix(residue, features), "samp") / row_total + ridge_term * weights
    chosen = jnp.take(probability, sampled)
    root_curv = jnp.sqrt(chosen * (1.0 - chosen))
    scaled = (jnp.take(features, sampled, axis=0) * root_curv[:, None]).astype(jnp.bfloat16)
    if paired:
        partner = partner_2(scaled, "feat", 0)
        joined = jnp.where(
            upper_side, jnp.concatenate([partner, scaled], 1), jnp.concatenate([scaled, partner], 1)
        )
        partial_gram = jnp.einsum("hb,hc->bc", joined, joined, preferred_element_type=jnp.float32)[
            None
        ]
    else:
        partial_gram = local_blocks(scaled)
    summed = lax.psum(partial_gram, "samp")
    gram = summed / hess_total + ridge_term * jnp.eye(BLK, dtype=jnp.float32)
    factors = jnp.linalg.cholesky(gram)

    def precondition(vector):
        if paired:
            other = partner_2(vector, "feat", 0)
            joined_vec = jnp.where(
                upper_side, jnp.concatenate([other, vector]), jnp.concatenate([vector, other])
            )[None]
            solved = block_solve(factors, joined_vec)[0]
            return jnp.where(upper_side, solved[columns:], solved[:columns])
        return block_solve(factors, vector.reshape(-1, BLK)).reshape(columns)

    def curvature(vector):
        image_rows = lax.psum(matrix_vector(scaled, vector), "feat")
        back = lax.psum(vector_matrix(image_rows, scaled), "samp")
        return back / hess_total + ridge_term * vector

    solution = jnp.zeros((columns,), jnp.float32)
    residual = -gradient

    def both_dots(resid_vec, precond_vec, image_vec):
        return lax.psum(
            (jnp.sum(resid_vec * precond_vec), jnp.sum(image_vec * precond_vec)), "feat"
        )

    precond = precondition(residual)
    image = curvature(precond)
    rz_now, wz_now = both_dots(residual, precond, image)
    alpha = rz_now / wz_now
    direction = precond
    along = image
    for iteration in range(ITERS):
        solution = solution + alpha * direction
        residual = residual - alpha * along
        if iteration + 1 < ITERS:
            precond = precondition(residual)
            image = curvature(precond)
            fresh, wz_now = both_dots(residual, precond, image)
            beta = fresh / rz_now
            alpha = fresh / (wz_now - beta * fresh / alpha)
            direction = precond + beta * direction
            along = image + beta * along
            rz_now = fresh
    return solution

def split_rows(row):
    top = row.astype(jnp.bfloat16).astype(jnp.float32)
    rest = row - top
    middle = rest.astype(jnp.bfloat16).astype(jnp.float32)
    bottom = rest - middle
    shape = (16, row.shape[1])
    line = lax.broadcasted_iota(jnp.int32, shape, 0)
    spread = lambda part: jnp.broadcast_to(part, shape)
    picked = jnp.where(
        line == 0,
        spread(top),
        jnp.where(line == 1, spread(middle), jnp.where(line == 2, spread(bottom), 0.0)),
    )
    return picked.astype(jnp.bfloat16)


def add_rows(parts):
    return parts[0:1] + parts[1:2] + parts[2:3]


def mxu(left, right, left_dim, right_dim):
    return lax.dot_general(
        left, right, (((left_dim,), (right_dim,)), ((), ())), preferred_element_type=jnp.float32
    )


def row_times(row, matrix):
    return add_rows(mxu(split_rows(row), matrix, 1, 0))


def row_times_transposed(row, matrix):
    return add_rows(mxu(split_rows(row), matrix, 1, 1))


def place():
    feat = lax.axis_index("feat")
    samp = lax.axis_index("samp")
    return feat // QUAD, feat % QUAD, samp


def greet(peers):
    barrier = pltpu.get_barrier_semaphore()
    for peer in peers:
        pl.semaphore_signal(barrier, inc=1, device_id=peer, device_id_type=MESH)
    return lambda: pl.semaphore_wait(barrier, len(peers))


def remote(source, target, send_sem, recv_sem, peer):
    return pltpu.make_async_remote_copy(
        src_ref=source,
        dst_ref=target,
        send_sem=send_sem,
        recv_sem=recv_sem,
        device_id=peer,
        device_id_type=MESH,
    )


def start_exchange(slots, mine, peers, send_sems, recv_sems):
    copies = []
    for number, peer in enumerate(peers):
        copy = remote(
            slots.at[mine], slots.at[mine], send_sems.at[number], recv_sems.at[number], peer
        )
        copy.start()
        copies.append(copy)
    return copies


def finish(copies):
    for copy in copies:
        copy.wait()


def total_of(slots, count):
    value = slots[0]
    for number in range(1, count):
        value = value + slots[number]
    return value


def quad_peers(depth, quarter, samp):
    return [{"feat": depth * QUAD + (quarter + k) % QUAD, "samp": samp} for k in range(1, QUAD)]


def depth_peers(layers, depth, quarter, samp):
    return [
        {"feat": ((depth + k) % layers) * QUAD + quarter, "samp": samp} for k in range(1, layers)
    ]


def plane_peers(depth, quarter, samp):
    member = samp * QUAD + quarter
    peers = []
    for k in range(1, 2 * QUAD):
        other = (member + k) % (2 * QUAD)
        peers.append({"feat": depth * QUAD + other % QUAD, "samp": other // QUAD})
    return peers


CHUNKS = 4


def gram_kernel(
    layers, features_home, weights, labels, sampled,
    scaled, gram, gradient,
    features, chosen, own_rows, sent_rows, came_rows, quad_slots, depth_slots, root_sent, root_came, grad_sent, grad_came,
    load_sem, ship_send, ship_recv, quad_send, quad_recv, depth_send, depth_recv, small_send, small_recv,
):
    depth, quarter, samp = place()
    rows, columns = features.shape
    samples = sampled.shape[1]
    half = columns // 2
    partner = {"feat": depth * QUAD + quarter, "samp": 1 - samp}
    across = quad_peers(depth, quarter, samp)
    along = depth_peers(layers, depth, quarter, samp)
    mine_at = pl.multiple_of(samp * half, 128)
    other_at = pl.multiple_of((1 - samp) * half, 128)
    piece = samples // CHUNKS

    def load(number, start):
        return pltpu.make_async_copy(
            features_home.at[:, pl.ds(start, half)],
            features.at[:, pl.ds(start, half)],
            load_sem.at[number],
        )

    load_other, load_mine = load(0, other_at), load(1, mine_at)
    load_other.start()
    load_mine.start()
    wait_all = greet([partner] + across + along)
    names = jnp.transpose(jnp.broadcast_to(sampled[...], (128, samples)))
    for start in range(0, rows, 128):
        number = lax.broadcasted_iota(jnp.int32, (samples, 128), 1) + start
        chosen[:, start : start + 128] = jnp.where(number == names, 1.0, 0.0).astype(jnp.bfloat16)
    load_other.wait()
    wait_all()

    def ship(number):
        first = number * piece
        return remote(
            sent_rows.at[pl.ds(first, piece)],
            came_rows.at[pl.ds(first, piece)],
            ship_send.at[number],
            ship_recv.at[number],
            partner,
        )

    def pick(number, carry):
        first = pl.multiple_of(number * piece, 128)
        sent_rows[pl.ds(first, piece), :] = mxu(
            chosen[pl.ds(first, piece), :], features[:, pl.ds(other_at, half)], 1, 0
        ).astype(jnp.bfloat16)
        ship(number).start()
        return carry

    lax.fori_loop(0, CHUNKS, pick, 0)
    load_mine.wait()
    quad_slots[quarter] = row_times_transposed(weights[...], features[...])
    quad_copies = start_exchange(quad_slots, quarter, across, quad_send, quad_recv)

    def pick_own(number, carry):
        first = pl.multiple_of(number * piece, 128)
        own_rows[pl.ds(first, piece), :] = mxu(
            chosen[pl.ds(first, piece), :], features[:, pl.ds(mine_at, half)], 1, 0
        ).astype(jnp.bfloat16)
        return carry

    finish(quad_copies)
    depth_slots[depth] = total_of(quad_slots, QUAD)
    depth_copies = start_exchange(depth_slots, depth, along, depth_send, depth_recv)
    lax.fori_loop(0, CHUNKS, pick_own, 0)
    finish(depth_copies)
    margin = total_of(depth_slots, layers)
    probability = 1.0 / (1.0 + jnp.exp(-margin))
    root = jnp.sqrt(probability * (1.0 - probability))
    own_root = row_times_transposed(root, chosen[...])
    root_sent[...] = own_root
    root_copy = remote(root_sent, root_came, small_send.at[0], small_recv.at[0], partner)
    root_copy.start()
    residue = probability - labels[...].astype(jnp.float32)
    grad_sent[...] = row_times(residue, features[:, pl.ds(other_at, half)])
    grad_copy = remote(grad_sent, grad_came, small_send.at[1], small_recv.at[1], partner)
    grad_copy.start()
    own_grad = row_times(residue, features[:, pl.ds(mine_at, half)])

    def scale_into(source, factor, first, start):
        for column in range(0, half, 128):
            wide = source[pl.ds(first, piece), column : column + 128].astype(jnp.float32) * factor
            scaled[pl.ds(start, piece), column : column + 128] = wide.astype(jnp.bfloat16)

    def root_factor(root_row, number):
        part = root_row[:, number * piece : (number + 1) * piece]
        return jnp.transpose(jnp.broadcast_to(part, (128, piece)))

    mine_row = pl.multiple_of(samp * samples, 128)
    other_row = pl.multiple_of((1 - samp) * samples, 128)
    for number in range(CHUNKS):
        first = number * piece
        scale_into(own_rows, root_factor(own_root, number), first, mine_row + first)
    own_block = scaled[pl.ds(mine_row, samples), :]
    gram[...] = mxu(own_block, own_block, 0, 0)
    for number in range(CHUNKS):
        first = number * piece
        ship(number).wait()
        if number == 0:
            root_copy.wait()
        scale_into(came_rows, root_factor(root_came[...], number), first, other_row + first)
        block = scaled[pl.ds(other_row + first, piece), :]
        gram[...] += mxu(block, block, 0, 0)
    ridge_term = RIDGE_COEF / F
    diagonal = lax.broadcasted_iota(jnp.int32, gram.shape, 0) == lax.broadcasted_iota(
        jnp.int32, gram.shape, 1
    )
    gram[...] = gram[...] / (2 * samples) + jnp.where(diagonal, ridge_term, 0.0)
    grad_copy.wait()
    gradient[...] = (own_grad + grad_came[...]) / (2 * rows) + ridge_term * weights[
        :, pl.ds(mine_at, half)
    ]


SQUARINGS = 6
POLISH = 2
LIMIT = 60


def halves(value):
    top = value.astype(jnp.bfloat16)
    return top, (value - top.astype(jnp.float32)).astype(jnp.bfloat16)


def inverse_kernel(gram, upper, lower, unit, inverse, pair):
    order = gram.shape[0]
    bound = jnp.max(jnp.sum(jnp.abs(gram[...]), axis=0, keepdims=True))
    shape = (order, order)
    eye = jnp.where(
        lax.broadcasted_iota(jnp.int32, shape, 0) == lax.broadcasted_iota(jnp.int32, shape, 1),
        1.0,
        0.0,
    )
    normed = gram[...] / bound
    unit[...] = normed
    power = eye - normed
    inverse[...] = eye + power

    first = power.astype(jnp.bfloat16)
    pair[:order] = mxu(first, first, 1, 0).astype(jnp.bfloat16)
    pair[order:] = inverse[...].astype(jnp.bfloat16)

    def square(_, carry):
        product = mxu(pair[...], pair[:order], 1, 0)
        value = inverse[...] + product[order:]
        inverse[...] = value
        pair[:order] = product[:order].astype(jnp.bfloat16)
        pair[order:] = value.astype(jnp.bfloat16)
        return carry

    lax.fori_loop(0, SQUARINGS - 1, square, 0)
    inverse[...] += mxu(pair[order:], pair[:order], 1, 0)
    unit_top, unit_low = halves(unit[...])

    def polish(_, size):
        value = inverse[...]
        top, low = halves(value)
        product = mxu(unit_top, top, 1, 0) + mxu(unit_top, low, 1, 0) + mxu(unit_low, top, 1, 0)
        left = eye - product
        inverse[...] = value + mxu(top, left.astype(jnp.bfloat16), 1, 0)
        return jnp.sum(left * left)

    size = lax.fori_loop(0, POLISH, polish, jnp.float32(0.0))
    settled = size < 0.0025

    @pl.when(jnp.logical_not(settled))
    def _():
        inverse[...] = eye

        def exact(left, right):
            return jnp.dot(
                left, right, precision=lax.Precision.HIGHEST, preferred_element_type=jnp.float32
            )

        def going(state):
            count, size_now = state
            return jnp.logical_and(count < LIMIT, size_now > 1e-8)

        def step(state):
            count, _ = state
            value = inverse[...]
            left = eye - exact(unit[...], value)
            fresh = value + exact(value, left)
            inverse[...] = 0.5 * (fresh + jnp.transpose(fresh))
            return count + 1, jnp.sum(left * left)

        lax.while_loop(going, step, (jnp.int32(0), jnp.float32(1.0)))

    top, low = halves(inverse[...] / bound)
    upper[...] = top
    lower[...] = low


def descent_kernel(
    layers, scaled, upper, lower, gradient,
    step,
    plane_slots, depth_slots, last_sent, last_came,
    plane_send, plane_recv, depth_send, depth_recv, last_send, last_recv,
):
    depth, quarter, samp = place()
    samples, half = scaled.shape
    partner = {"feat": depth * QUAD + quarter, "samp": 1 - samp}
    plane = plane_peers(depth, quarter, samp)
    along = depth_peers(layers, depth, quarter, samp)
    wait_all = greet(plane + along)
    member = samp * QUAD + quarter
    ridge_term = RIDGE_COEF / F
    lane = lax.broadcasted_iota(jnp.int32, (1, 128), 1)

    def precondition(vector):
        parts = split_rows(vector)
        return add_rows(mxu(parts, upper[...], 1, 0) + mxu(parts, lower[...], 1, 0))

    def total(row):
        return jnp.sum(row, axis=1, keepdims=True)

    residual = -gradient[...]
    answer = jnp.zeros_like(residual)
    direction = jnp.zeros_like(residual)
    along_rows = None
    rz_now = None
    length = None
    for iteration in range(ITERS):
        precond = precondition(residual)
        numbers = jnp.where(
            lane == 0,
            total(residual * precond),
            jnp.where(
                lane == 1,
                total(precond * precond),
                jnp.where(lane == 2, total(precond * direction), 0.0),
            ),
        )
        mine = plane_slots.at[iteration, member]
        mine[:, :samples] = row_times_transposed(precond, scaled[...])
        mine[:, samples:] = numbers
        if iteration == 0:
            wait_all()
        finish(
            start_exchange(
                plane_slots.at[iteration], member, plane, plane_send.at[iteration], plane_recv.at[iteration]
            )
        )
        depth_slots[iteration, depth] = total_of(plane_slots.at[iteration], 2 * QUAD)
        finish(
            start_exchange(
                depth_slots.at[iteration], depth, along, depth_send.at[iteration], depth_recv.at[iteration]
            )
        )
        summed = total_of(depth_slots.at[iteration], layers)
        image_rows = summed[:, :samples]
        fresh = summed[:, samples : samples + 1]
        square = summed[:, samples + 1 : samples + 2]
        cross = summed[:, samples + 2 : samples + 3]
        if iteration == 0:
            direction = precond
            along_rows = image_rows
            length = square
        else:
            beta = fresh / rz_now
            direction = precond + beta * direction
            along_rows = image_rows + beta * along_rows
            length = square + 2.0 * beta * cross + beta * beta * length
        rz_now = fresh
        alpha = rz_now / (total(along_rows * along_rows) / samples + ridge_term * length)
        answer = answer + alpha * direction
        if iteration + 1 < ITERS:
            image = row_times(along_rows, scaled[...]) / samples + ridge_term * direction
            residual = residual - alpha * image
    last_sent[...] = answer
    final = remote(last_sent, last_came, last_send.at[0], last_recv.at[0], partner)
    final.start()
    step[:, pl.ds(pl.multiple_of(samp * half, 128), half)] = answer
    final.wait()
    step[:, pl.ds(pl.multiple_of((1 - samp) * half, 128), half)] = last_came[...]


def split_device(features, labels, weights, sampled):
    rows, columns = features.shape
    samples = sampled.shape[0]
    half = columns // 2
    layers = lax.axis_size("feat") // QUAD
    shaped = jax.ShapeDtypeStruct
    whole = pl.BlockSpec(memory_space=pltpu.VMEM)
    dma = pltpu.SemaphoreType.DMA
    vmem = pltpu.VMEM
    scaled, gram, gradient = pl.pallas_call(
        functools.partial(gram_kernel, layers),
        out_shape=(
            shaped((2 * samples, half), jnp.bfloat16),
            shaped((half, half), jnp.float32),
            shaped((1, half), jnp.float32),
        ),
        in_specs=[pl.BlockSpec(memory_space=pl.ANY)] + [whole] * 3,
        out_specs=(whole,) * 3,
        scratch_shapes=[
            vmem((rows, columns), jnp.bfloat16),
            vmem((samples, rows), jnp.bfloat16),
            vmem((samples, half), jnp.bfloat16),
            vmem((samples, half), jnp.bfloat16),
            vmem((samples, half), jnp.bfloat16),
            vmem((QUAD, 1, rows), jnp.float32),
            vmem((layers, 1, rows), jnp.float32),
            vmem((1, samples), jnp.float32),
            vmem((1, samples), jnp.float32),
            vmem((1, half), jnp.float32),
            vmem((1, half), jnp.float32),
            dma((2,)),
            dma((CHUNKS,)),
            dma((CHUNKS,)),
            dma((QUAD - 1,)),
            dma((QUAD - 1,)),
            dma((layers - 1,)),
            dma((layers - 1,)),
            dma((2,)),
            dma((2,)),
        ],
        compiler_params=pltpu.CompilerParams(collective_id=0, has_side_effects=True),
    )(features, weights[None, :], labels[None, :], sampled[None, :])
    upper, lower = pl.pallas_call(
        inverse_kernel,
        out_shape=(shaped((half, half), jnp.bfloat16),) * 2,
        in_specs=[whole],
        out_specs=(whole,) * 2,
        scratch_shapes=[
            vmem((half, half), jnp.float32),
            vmem((half, half), jnp.float32),
            vmem((2 * half, half), jnp.bfloat16),
        ],
    )(gram)
    width = 2 * samples + 128
    step = pl.pallas_call(
        functools.partial(descent_kernel, layers),
        out_shape=shaped((1, columns), jnp.float32),
        in_specs=[whole] * 4,
        out_specs=whole,
        scratch_shapes=[
            vmem((ITERS, 2 * QUAD, 1, width), jnp.float32),
            vmem((ITERS, layers, 1, width), jnp.float32),
            vmem((1, half), jnp.float32),
            vmem((1, half), jnp.float32),
            dma((ITERS, 2 * QUAD - 1)),
            dma((ITERS, 2 * QUAD - 1)),
            dma((ITERS, layers - 1)),
            dma((ITERS, layers - 1)),
            dma((1,)),
            dma((1,)),
        ],
        compiler_params=pltpu.CompilerParams(collective_id=1, has_side_effects=True),
    )(scaled, upper, lower, gradient)
    return step[0]


def solution(mesh):
    placed = (P("samp", "feat"), P("samp"), P("feat"), P("samp"))
    devices, groups = mesh.shape["feat"], mesh.shape["samp"]
    apart = groups == 2 and devices % QUAD == 0 and devices > QUAD and F // devices == 2 * BLK
    return jax.shard_map(
        split_device if apart else per_device,
        mesh=mesh,
        in_specs=placed,
        out_specs=P("feat"),
        check_vma=False,
    )
```

```python
import functools

import jax
import jax.numpy as jnp
from jax import lax
from jax.experimental import pallas as pl
from jax.experimental.pallas import tpu as pltpu
from jax.sharding import PartitionSpec as P

F = 16384
BLK = 512
ITERS = 3
QUAD = 4
MESH = pl.DeviceIdType.MESH


RIDGE_COEF = 0.05


def partner_2(value, axis, apart):
    mask = 2**apart
    pairs = [(source, source ^ mask) for source in range(lax.axis_size(axis))]
    return lax.ppermute(value, axis, pairs)


def split_parts(vector):
    upper_part = vector.astype(jnp.bfloat16)
    widened = lax.optimization_barrier(upper_part).astype(jnp.float32)
    lower_part = (vector - widened).astype(jnp.bfloat16)
    return (upper_part, lower_part)


def matrix_vector(matrix, vector):
    upper_part, lower_part = split_parts(vector)
    return jnp.dot(matrix, upper_part, preferred_element_type=jnp.float32) + jnp.dot(
        matrix, lower_part, preferred_element_type=jnp.float32
    )


def vector_matrix(vector, matrix):
    upper_part, lower_part = split_parts(vector)
    return jnp.dot(upper_part, matrix, preferred_element_type=jnp.float32) + jnp.dot(
        lower_part, matrix, preferred_element_type=jnp.float32
    )


def block_solve(factors, rhs_blocks):
    forward = jax.vmap(
        lambda factor, column: jax.scipy.linalg.solve_triangular(factor, column, lower=True)
    )(factors, rhs_blocks)
    return jax.vmap(
        lambda factor, column: jax.scipy.linalg.solve_triangular(
            factor, column, lower=True, trans=1
        )
    )(factors, forward)


def local_blocks(scaled):
    blocks = scaled.reshape(scaled.shape[0], scaled.shape[1] // BLK, BLK)
    return jnp.einsum("hkb,hkc->kbc", blocks, blocks, preferred_element_type=jnp.float32)


def per_device(features, labels, weights, sampled):
    columns = features.shape[1]
    sample_rows = sampled.shape[0]
    groups = lax.axis_size("samp")
    row_total = features.shape[0] * groups
    hess_total = sample_rows * groups
    ridge_term = RIDGE_COEF / F
    paired = columns < BLK
    upper_side = lax.axis_index("feat") % 2 == 1
    margin = lax.psum(matrix_vector(features, weights), "feat")
    probability = jax.nn.sigmoid(margin)
    residue = probability - labels.astype(jnp.float32)
    gradient = lax.psum(vector_matrix(residue, features), "samp") / row_total + ridge_term * weights
    chosen = jnp.take(probability, sampled)
    root_curv = jnp.sqrt(chosen * (1.0 - chosen))
    scaled = (jnp.take(features, sampled, axis=0) * root_curv[:, None]).astype(jnp.bfloat16)
    if paired:
        partner = partner_2(scaled, "feat", 0)
        joined = jnp.where(
            upper_side, jnp.concatenate([partner, scaled], 1), jnp.concatenate([scaled, partner], 1)
        )
        partial_gram = jnp.einsum("hb,hc->bc", joined, joined, preferred_element_type=jnp.float32)[
            None
        ]
    else:
        partial_gram = local_blocks(scaled)
    summed = lax.psum(partial_gram, "samp")
    gram = summed / hess_total + ridge_term * jnp.eye(BLK, dtype=jnp.float32)
    factors = jnp.linalg.cholesky(gram)

    def precondition(vector):
        if paired:
            other = partner_2(vector, "feat", 0)
            joined_vec = jnp.where(
                upper_side, jnp.concatenate([other, vector]), jnp.concatenate([vector, other])
            )[None]
            solved = block_solve(factors, joined_vec)[0]
            return jnp.where(upper_side, solved[columns:], solved[:columns])
        return block_solve(factors, vector.reshape(-1, BLK)).reshape(columns)

    def curvature(vector):
        image_rows = lax.psum(matrix_vector(scaled, vector), "feat")
        back = lax.psum(vector_matrix(image_rows, scaled), "samp")
        return back / hess_total + ridge_term * vector

    solution = jnp.zeros((columns,), jnp.float32)
    residual = -gradient

    def both_dots(resid_vec, precond_vec, image_vec):
        return lax.psum(
            (jnp.sum(resid_vec * precond_vec), jnp.sum(image_vec * precond_vec)), "feat"
        )

    precond = precondition(residual)
    image = curvature(precond)
    rz_now, wz_now = both_dots(residual, precond, image)
    alpha = rz_now / wz_now
    direction = precond
    along = image
    for iteration in range(ITERS):
        solution = solution + alpha * direction
        residual = residual - alpha * along
        if iteration + 1 < ITERS:
            precond = precondition(residual)
            image = curvature(precond)
            fresh, wz_now = both_dots(residual, precond, image)
            beta = fresh / rz_now
            alpha = fresh / (wz_now - beta * fresh / alpha)
            direction = precond + beta * direction
            along = image + beta * along
            rz_now = fresh
    return solution

def split_rows(row):
    top = row.astype(jnp.bfloat16).astype(jnp.float32)
    rest = row - top
    middle = rest.astype(jnp.bfloat16).astype(jnp.float32)
    bottom = rest - middle
    shape = (16, row.shape[1])
    line = lax.broadcasted_iota(jnp.int32, shape, 0)
    spread = lambda part: jnp.broadcast_to(part, shape)
    picked = jnp.where(
        line == 0,
        spread(top),
        jnp.where(line == 1, spread(middle), jnp.where(line == 2, spread(bottom), 0.0)),
    )
    return picked.astype(jnp.bfloat16)


def add_rows(parts):
    return parts[0:1] + parts[1:2] + parts[2:3]


def mxu(left, right, left_dim, right_dim):
    return lax.dot_general(
        left, right, (((left_dim,), (right_dim,)), ((), ())), preferred_element_type=jnp.float32
    )


def row_times(row, matrix):
    return add_rows(mxu(split_rows(row), matrix, 1, 0))


def row_times_transposed(row, matrix):
    return add_rows(mxu(split_rows(row), matrix, 1, 1))


def place():
    feat = lax.axis_index("feat")
    samp = lax.axis_index("samp")
    return feat // QUAD, feat % QUAD, samp


def greet(peers):
    barrier = pltpu.get_barrier_semaphore()
    for peer in peers:
        pl.semaphore_signal(barrier, inc=1, device_id=peer, device_id_type=MESH)
    return lambda: pl.semaphore_wait(barrier, len(peers))


def remote(source, target, send_sem, recv_sem, peer):
    return pltpu.make_async_remote_copy(
        src_ref=source,
        dst_ref=target,
        send_sem=send_sem,
        recv_sem=recv_sem,
        device_id=peer,
        device_id_type=MESH,
    )


def start_exchange(slots, mine, peers, send_sems, recv_sems):
    copies = []
    for number, peer in enumerate(peers):
        copy = remote(
            slots.at[mine], slots.at[mine], send_sems.at[number], recv_sems.at[number], peer
        )
        copy.start()
        copies.append(copy)
    return copies


def finish(copies):
    for copy in copies:
        copy.wait()


def total_of(slots, count):
    value = slots[0]
    for number in range(1, count):
        value = value + slots[number]
    return value


def quad_peers(depth, quarter, samp):
    return [{"feat": depth * QUAD + (quarter + k) % QUAD, "samp": samp} for k in range(1, QUAD)]


def depth_peers(layers, depth, quarter, samp):
    return [
        {"feat": ((depth + k) % layers) * QUAD + quarter, "samp": samp} for k in range(1, layers)
    ]


def plane_peers(depth, quarter, samp):
    member = samp * QUAD + quarter
    peers = []
    for k in range(1, 2 * QUAD):
        other = (member + k) % (2 * QUAD)
        peers.append({"feat": depth * QUAD + other % QUAD, "samp": other // QUAD})
    return peers


CHUNKS = 4


def gram_kernel(
    layers, features_home, weights, labels, sampled,
    scaled_home, gram_home, gradient, upper, lower, size,
    scaled, gram, inverse, pair, features, chosen, own_rows, sent_rows, came_rows, quad_slots, depth_slots, root_sent, root_came, grad_sent, grad_came,
    load_sem, store_sem, ship_send, ship_recv, quad_send, quad_recv, depth_send, depth_recv, small_send, small_recv,
):
    depth, quarter, samp = place()
    rows, columns = features.shape
    samples = sampled.shape[1]
    half = columns // 2
    partner = {"feat": depth * QUAD + quarter, "samp": 1 - samp}
    across = quad_peers(depth, quarter, samp)
    along = depth_peers(layers, depth, quarter, samp)
    mine_at = pl.multiple_of(samp * half, 128)
    other_at = pl.multiple_of((1 - samp) * half, 128)
    piece = samples // CHUNKS

    def load(number, start):
        return pltpu.make_async_copy(
            features_home.at[:, pl.ds(start, half)],
            features.at[:, pl.ds(start, half)],
            load_sem.at[number],
        )

    load_other, load_mine = load(0, other_at), load(1, mine_at)
    load_other.start()
    load_mine.start()
    wait_all = greet([partner] + across + along)
    names = jnp.transpose(jnp.broadcast_to(sampled[...], (128, samples)))
    for start in range(0, rows, 128):
        number = lax.broadcasted_iota(jnp.int32, (samples, 128), 1) + start
        chosen[:, start : start + 128] = jnp.where(number == names, 1.0, 0.0).astype(jnp.bfloat16)
    load_other.wait()
    wait_all()

    def ship(number):
        first = number * piece
        return remote(
            sent_rows.at[pl.ds(first, piece)],
            came_rows.at[pl.ds(first, piece)],
            ship_send.at[number],
            ship_recv.at[number],
            partner,
        )

    def pick(number, carry):
        first = pl.multiple_of(number * piece, 128)
        sent_rows[pl.ds(first, piece), :] = mxu(
            chosen[pl.ds(first, piece), :], features[:, pl.ds(other_at, half)], 1, 0
        ).astype(jnp.bfloat16)
        ship(number).start()
        return carry

    lax.fori_loop(0, CHUNKS, pick, 0)
    load_mine.wait()
    quad_slots[quarter] = row_times_transposed(weights[...], features[...])
    quad_copies = start_exchange(quad_slots, quarter, across, quad_send, quad_recv)

    def pick_own(number, carry):
        first = pl.multiple_of(number * piece, 128)
        own_rows[pl.ds(first, piece), :] = mxu(
            chosen[pl.ds(first, piece), :], features[:, pl.ds(mine_at, half)], 1, 0
        ).astype(jnp.bfloat16)
        return carry

    finish(quad_copies)
    depth_slots[depth] = total_of(quad_slots, QUAD)
    depth_copies = start_exchange(depth_slots, depth, along, depth_send, depth_recv)
    lax.fori_loop(0, CHUNKS, pick_own, 0)
    finish(depth_copies)
    margin = total_of(depth_slots, layers)
    probability = 1.0 / (1.0 + jnp.exp(-margin))
    root = jnp.sqrt(probability * (1.0 - probability))
    own_root = row_times_transposed(root, chosen[...])
    root_sent[...] = own_root
    root_copy = remote(root_sent, root_came, small_send.at[0], small_recv.at[0], partner)
    root_copy.start()
    residue = probability - labels[...].astype(jnp.float32)
    grad_sent[...] = row_times(residue, features[:, pl.ds(other_at, half)])
    grad_copy = remote(grad_sent, grad_came, small_send.at[1], small_recv.at[1], partner)
    grad_copy.start()
    own_grad = row_times(residue, features[:, pl.ds(mine_at, half)])

    def scale_into(source, factor, first, start):
        for column in range(0, half, 128):
            wide = source[pl.ds(first, piece), column : column + 128].astype(jnp.float32) * factor
            scaled[pl.ds(start, piece), column : column + 128] = wide.astype(jnp.bfloat16)

    def root_factor(root_row, number):
        part = root_row[:, number * piece : (number + 1) * piece]
        return jnp.transpose(jnp.broadcast_to(part, (128, piece)))

    mine_row = pl.multiple_of(samp * samples, 128)
    other_row = pl.multiple_of((1 - samp) * samples, 128)
    for number in range(CHUNKS):
        first = number * piece
        scale_into(own_rows, root_factor(own_root, number), first, mine_row + first)
    stores = [
        pltpu.make_async_copy(
            scaled.at[pl.ds(mine_row, samples)],
            scaled_home.at[pl.ds(mine_row, samples)],
            store_sem.at[CHUNKS],
        )
    ]
    stores[0].start()
    own_block = scaled[pl.ds(mine_row, samples), :]
    gram[...] = mxu(own_block, own_block, 0, 0)
    ridge_term = RIDGE_COEF / F
    shape = gram.shape
    same = lax.broadcasted_iota(jnp.int32, shape, 0) == lax.broadcasted_iota(jnp.int32, shape, 1)
    eye = jnp.where(same, 1.0, 0.0)
    bound = None
    for number in range(CHUNKS):
        first = number * piece
        if number == CHUNKS - 1:
            bound = early_inverse(gram[...] / (samples + first) + ridge_term * eye, eye, inverse, pair)
        ship(number).wait()
        if number == 0:
            root_copy.wait()
        scale_into(came_rows, root_factor(root_came[...], number), first, other_row + first)
        store = pltpu.make_async_copy(
            scaled.at[pl.ds(other_row + first, piece)],
            scaled_home.at[pl.ds(other_row + first, piece)],
            store_sem.at[number],
        )
        store.start()
        stores.append(store)
        block = scaled[pl.ds(other_row + first, piece), :]
        gram[...] += mxu(block, block, 0, 0)
    gram[...] = gram[...] / (2 * samples) + ridge_term * eye
    store = pltpu.make_async_copy(gram, gram_home, store_sem.at[CHUNKS + 1])
    store.start()
    stores.append(store)
    size[...] = jnp.broadcast_to(late_inverse(gram, bound, eye, inverse, pair, upper, lower), (1, 128))
    grad_copy.wait()
    gradient[...] = (own_grad + grad_came[...]) / (2 * rows) + ridge_term * weights[
        :, pl.ds(mine_at, half)
    ]
    for store in stores:
        store.wait()


SQUARINGS = 6
POLISH = 2
LIMIT = 60
DAMP = 0.75
SETTLED = 0.0025


def halves(value):
    top = value.astype(jnp.bfloat16)
    return top, (value - top.astype(jnp.float32)).astype(jnp.bfloat16)


def raise_power(inverse, pair, count):
    order = inverse.shape[0]

    def square(_, carry):
        product = mxu(pair[...], pair[:order], 1, 0)
        value = inverse[...] + product[order:]
        inverse[...] = value
        pair[:order] = product[:order].astype(jnp.bfloat16)
        pair[order:] = value.astype(jnp.bfloat16)
        return carry

    lax.fori_loop(0, count - 1, square, 0)
    inverse[...] += mxu(pair[order:], pair[:order], 1, 0)


def early_inverse(early, eye, inverse, pair):
    order = early.shape[0]
    bound = jnp.max(jnp.sum(jnp.abs(early), axis=0, keepdims=True), axis=1, keepdims=True)
    power = eye - early / bound
    value = eye + power
    inverse[...] = value
    first = power.astype(jnp.bfloat16)
    pair[:order] = mxu(first, first, 1, 0).astype(jnp.bfloat16)
    pair[order:] = value.astype(jnp.bfloat16)
    raise_power(inverse, pair, SQUARINGS)
    return bound


def late_inverse(gram, bound, eye, inverse, pair, upper, lower):
    order = gram.shape[0]
    unit_top, unit_low = halves(gram[...] / bound)
    value = DAMP * inverse[...]
    inverse[...] = value
    top = value.astype(jnp.bfloat16)
    pair[order:] = top
    pair[:order] = (eye - mxu(unit_top, top, 1, 0)).astype(jnp.bfloat16)
    raise_power(inverse, pair, 2)
    left = None
    for _ in range(POLISH):
        value = inverse[...]
        top, low = halves(value)
        product = mxu(unit_top, top, 1, 0) + mxu(unit_top, low, 1, 0) + mxu(unit_low, top, 1, 0)
        left = eye - product
        inverse[...] = value + mxu(top, left.astype(jnp.bfloat16), 1, 0)
    top, low = halves(inverse[...] / bound)
    upper[...] = top
    lower[...] = low
    return jnp.sum(jnp.sum(left * left, axis=0, keepdims=True), axis=1, keepdims=True)


def rescue_kernel(size, gram_home, _upper, _lower, upper_home, lower_home, unit, inverse, top_half, low_half):
    settled = size[0, 0] < SETTLED

    @pl.when(jnp.logical_not(settled))
    def _():
        pltpu.sync_copy(gram_home, unit)
        bound = jnp.max(jnp.sum(jnp.abs(unit[...]), axis=0, keepdims=True))
        unit[...] = unit[...] / bound
        shape = unit.shape
        eye = jnp.where(
            lax.broadcasted_iota(jnp.int32, shape, 0) == lax.broadcasted_iota(jnp.int32, shape, 1),
            1.0,
            0.0,
        )
        inverse[...] = eye

        def exact(left, right):
            return jnp.dot(
                left, right, precision=lax.Precision.HIGHEST, preferred_element_type=jnp.float32
            )

        def going(state):
            count, size_now = state
            return jnp.logical_and(count < LIMIT, size_now > 1e-8)

        def step(state):
            count, _ = state
            value = inverse[...]
            left = eye - exact(unit[...], value)
            fresh = value + exact(value, left)
            inverse[...] = 0.5 * (fresh + jnp.transpose(fresh))
            return count + 1, jnp.sum(left * left)

        lax.while_loop(going, step, (jnp.int32(0), jnp.float32(1.0)))
        top, low = halves(inverse[...] / bound)
        top_half[...] = top
        low_half[...] = low
        pltpu.sync_copy(top_half, upper_home)
        pltpu.sync_copy(low_half, lower_home)


def descent_kernel(
    layers, scaled_home, upper, lower, gradient,
    step,
    scaled, plane_slots, depth_slots, part_sent, part_came,
    load_sem, plane_send, plane_recv, depth_send, depth_recv, part_send, part_recv,
):
    depth, quarter, samp = place()
    samples, half = scaled.shape
    partner = {"feat": depth * QUAD + quarter, "samp": 1 - samp}
    plane = plane_peers(depth, quarter, samp)
    along = depth_peers(layers, depth, quarter, samp)
    load = pltpu.make_async_copy(scaled_home, scaled, load_sem.at[0])
    load.start()
    wait_all = greet(plane + along)
    member = samp * QUAD + quarter
    ridge_term = RIDGE_COEF / F
    lane = lax.broadcasted_iota(jnp.int32, (1, 128), 1)

    def precondition(vector):
        parts = split_rows(vector)
        return add_rows(mxu(parts, upper[...], 1, 0) + mxu(parts, lower[...], 1, 0))

    def total(row):
        return jnp.sum(row, axis=1, keepdims=True)

    residual = -gradient[...]
    answer = jnp.zeros_like(residual)
    direction = jnp.zeros_like(residual)
    twin_answer = jnp.zeros_like(residual)
    twin_direction = jnp.zeros_like(residual)
    along_rows = None
    rz_now = None
    length = None
    for iteration in range(ITERS):
        precond = precondition(residual)
        numbers = jnp.where(
            lane == 0,
            total(residual * precond),
            jnp.where(
                lane == 1,
                total(precond * precond),
                jnp.where(lane == 2, total(precond * direction), 0.0),
            ),
        )
        mine = plane_slots.at[iteration, member]
        part_sent[iteration] = precond
        if iteration == 0:
            load.wait()
        mine[:, :samples] = row_times_transposed(precond, scaled[...])
        mine[:, samples:] = numbers
        if iteration == 0:
            wait_all()
        plane_copies = start_exchange(
            plane_slots.at[iteration], member, plane, plane_send.at[iteration], plane_recv.at[iteration]
        )
        twin_copy = remote(
            part_sent.at[iteration],
            part_came.at[iteration],
            part_send.at[iteration],
            part_recv.at[iteration],
            partner,
        )
        twin_copy.start()
        finish(plane_copies)
        depth_slots[iteration, depth] = total_of(plane_slots.at[iteration], 2 * QUAD)
        finish(
            start_exchange(
                depth_slots.at[iteration], depth, along, depth_send.at[iteration], depth_recv.at[iteration]
            )
        )
        twin_copy.wait()
        twin_precond = part_came[iteration]
        summed = total_of(depth_slots.at[iteration], layers)
        image_rows = summed[:, :samples]
        fresh = summed[:, samples : samples + 1]
        square = summed[:, samples + 1 : samples + 2]
        cross = summed[:, samples + 2 : samples + 3]
        if iteration == 0:
            direction = precond
            twin_direction = twin_precond
            along_rows = image_rows
            length = square
        else:
            beta = fresh / rz_now
            direction = precond + beta * direction
            twin_direction = twin_precond + beta * twin_direction
            along_rows = image_rows + beta * along_rows
            length = square + 2.0 * beta * cross + beta * beta * length
        rz_now = fresh
        alpha = rz_now / (total(along_rows * along_rows) / samples + ridge_term * length)
        answer = answer + alpha * direction
        twin_answer = twin_answer + alpha * twin_direction
        if iteration + 1 < ITERS:
            image = row_times(along_rows, scaled[...]) / samples + ridge_term * direction
            residual = residual - alpha * image
    step[:, pl.ds(pl.multiple_of(samp * half, 128), half)] = answer
    step[:, pl.ds(pl.multiple_of((1 - samp) * half, 128), half)] = twin_answer


def split_device(features, labels, weights, sampled):
    rows, columns = features.shape
    samples = sampled.shape[0]
    half = columns // 2
    layers = lax.axis_size("feat") // QUAD
    shaped = jax.ShapeDtypeStruct
    whole = pl.BlockSpec(memory_space=pltpu.VMEM)
    dma = pltpu.SemaphoreType.DMA
    vmem = pltpu.VMEM
    anywhere = pl.BlockSpec(memory_space=pl.ANY)
    scaled, gram, gradient, upper, lower, size = pl.pallas_call(
        functools.partial(gram_kernel, layers),
        out_shape=(
            shaped((2 * samples, half), jnp.bfloat16),
            shaped((half, half), jnp.float32),
            shaped((1, half), jnp.float32),
            shaped((half, half), jnp.bfloat16),
            shaped((half, half), jnp.bfloat16),
            shaped((1, 128), jnp.float32),
        ),
        in_specs=[anywhere] + [whole] * 3,
        out_specs=(anywhere,) * 2 + (whole,) * 4,
        scratch_shapes=[
            vmem((2 * samples, half), jnp.bfloat16),
            vmem((half, half), jnp.float32),
            vmem((half, half), jnp.float32),
            vmem((2 * half, half), jnp.bfloat16),
            vmem((rows, columns), jnp.bfloat16),
            vmem((samples, rows), jnp.bfloat16),
            vmem((samples, half), jnp.bfloat16),
            vmem((samples, half), jnp.bfloat16),
            vmem((samples, half), jnp.bfloat16),
            vmem((QUAD, 1, rows), jnp.float32),
            vmem((layers, 1, rows), jnp.float32),
            vmem((1, samples), jnp.float32),
            vmem((1, samples), jnp.float32),
            vmem((1, half), jnp.float32),
            vmem((1, half), jnp.float32),
            dma((2,)),
            dma((CHUNKS + 2,)),
            dma((CHUNKS,)),
            dma((CHUNKS,)),
            dma((QUAD - 1,)),
            dma((QUAD - 1,)),
            dma((layers - 1,)),
            dma((layers - 1,)),
            dma((2,)),
            dma((2,)),
        ],
        compiler_params=pltpu.CompilerParams(collective_id=0, has_side_effects=True),
    )(features, weights[None, :], labels[None, :], sampled[None, :])
    upper, lower = pl.pallas_call(
        rescue_kernel,
        out_shape=(shaped((half, half), jnp.bfloat16),) * 2,
        in_specs=[pl.BlockSpec(memory_space=pltpu.SMEM)] + [anywhere] * 3,
        out_specs=(anywhere,) * 2,
        scratch_shapes=[
            vmem((half, half), jnp.float32),
            vmem((half, half), jnp.float32),
            vmem((half, half), jnp.bfloat16),
            vmem((half, half), jnp.bfloat16),
        ],
        input_output_aliases={2: 0, 3: 1},
    )(size, gram, upper, lower)
    width = 2 * samples + 128
    step = pl.pallas_call(
        functools.partial(descent_kernel, layers),
        out_shape=shaped((1, columns), jnp.float32),
        in_specs=[anywhere] + [whole] * 3,
        out_specs=whole,
        scratch_shapes=[
            vmem((2 * samples, half), jnp.bfloat16),
            vmem((ITERS, 2 * QUAD, 1, width), jnp.float32),
            vmem((ITERS, layers, 1, width), jnp.float32),
            vmem((ITERS, 1, half), jnp.float32),
            vmem((ITERS, 1, half), jnp.float32),
            dma((1,)),
            dma((ITERS, 2 * QUAD - 1)),
            dma((ITERS, 2 * QUAD - 1)),
            dma((ITERS, layers - 1)),
            dma((ITERS, layers - 1)),
            dma((ITERS,)),
            dma((ITERS,)),
        ],
        compiler_params=pltpu.CompilerParams(collective_id=1, has_side_effects=True),
    )(scaled, upper, lower, gradient)
    return step[0]


def solution(mesh):
    placed = (P("samp", "feat"), P("samp"), P("feat"), P("samp"))
    devices, groups = mesh.shape["feat"], mesh.shape["samp"]
    apart = groups == 2 and devices % QUAD == 0 and devices > QUAD and F // devices == 2 * BLK
    return jax.shard_map(
        split_device if apart else per_device,
        mesh=mesh,
        in_specs=placed,
        out_specs=P("feat"),
        check_vma=False,
    )
```

```python
import functools

import jax
import jax.numpy as jnp
from jax import lax
from jax.experimental import pallas as pl
from jax.experimental.pallas import tpu as pltpu
from jax.sharding import PartitionSpec as P

F = 16384
BLK = 512
ITERS = 3
QUAD = 4
MESH = pl.DeviceIdType.MESH


RIDGE_COEF = 0.05


def partner_2(value, axis, apart):
    mask = 2**apart
    pairs = [(source, source ^ mask) for source in range(lax.axis_size(axis))]
    return lax.ppermute(value, axis, pairs)


def split_parts(vector):
    upper_part = vector.astype(jnp.bfloat16)
    widened = lax.optimization_barrier(upper_part).astype(jnp.float32)
    lower_part = (vector - widened).astype(jnp.bfloat16)
    return (upper_part, lower_part)


def matrix_vector(matrix, vector):
    upper_part, lower_part = split_parts(vector)
    return jnp.dot(matrix, upper_part, preferred_element_type=jnp.float32) + jnp.dot(
        matrix, lower_part, preferred_element_type=jnp.float32
    )


def vector_matrix(vector, matrix):
    upper_part, lower_part = split_parts(vector)
    return jnp.dot(upper_part, matrix, preferred_element_type=jnp.float32) + jnp.dot(
        lower_part, matrix, preferred_element_type=jnp.float32
    )


def block_solve(factors, rhs_blocks):
    forward = jax.vmap(
        lambda factor, column: jax.scipy.linalg.solve_triangular(factor, column, lower=True)
    )(factors, rhs_blocks)
    return jax.vmap(
        lambda factor, column: jax.scipy.linalg.solve_triangular(
            factor, column, lower=True, trans=1
        )
    )(factors, forward)


def local_blocks(scaled):
    blocks = scaled.reshape(scaled.shape[0], scaled.shape[1] // BLK, BLK)
    return jnp.einsum("hkb,hkc->kbc", blocks, blocks, preferred_element_type=jnp.float32)


def per_device(features, labels, weights, sampled):
    columns = features.shape[1]
    sample_rows = sampled.shape[0]
    groups = lax.axis_size("samp")
    row_total = features.shape[0] * groups
    hess_total = sample_rows * groups
    ridge_term = RIDGE_COEF / F
    paired = columns < BLK
    upper_side = lax.axis_index("feat") % 2 == 1
    margin = lax.psum(matrix_vector(features, weights), "feat")
    probability = jax.nn.sigmoid(margin)
    residue = probability - labels.astype(jnp.float32)
    gradient = lax.psum(vector_matrix(residue, features), "samp") / row_total + ridge_term * weights
    chosen = jnp.take(probability, sampled)
    root_curv = jnp.sqrt(chosen * (1.0 - chosen))
    scaled = (jnp.take(features, sampled, axis=0) * root_curv[:, None]).astype(jnp.bfloat16)
    if paired:
        partner = partner_2(scaled, "feat", 0)
        joined = jnp.where(
            upper_side, jnp.concatenate([partner, scaled], 1), jnp.concatenate([scaled, partner], 1)
        )
        partial_gram = jnp.einsum("hb,hc->bc", joined, joined, preferred_element_type=jnp.float32)[
            None
        ]
    else:
        partial_gram = local_blocks(scaled)
    summed = lax.psum(partial_gram, "samp")
    gram = summed / hess_total + ridge_term * jnp.eye(BLK, dtype=jnp.float32)
    factors = jnp.linalg.cholesky(gram)

    def precondition(vector):
        if paired:
            other = partner_2(vector, "feat", 0)
            joined_vec = jnp.where(
                upper_side, jnp.concatenate([other, vector]), jnp.concatenate([vector, other])
            )[None]
            solved = block_solve(factors, joined_vec)[0]
            return jnp.where(upper_side, solved[columns:], solved[:columns])
        return block_solve(factors, vector.reshape(-1, BLK)).reshape(columns)

    def curvature(vector):
        image_rows = lax.psum(matrix_vector(scaled, vector), "feat")
        back = lax.psum(vector_matrix(image_rows, scaled), "samp")
        return back / hess_total + ridge_term * vector

    solution = jnp.zeros((columns,), jnp.float32)
    residual = -gradient

    def both_dots(resid_vec, precond_vec, image_vec):
        return lax.psum(
            (jnp.sum(resid_vec * precond_vec), jnp.sum(image_vec * precond_vec)), "feat"
        )

    precond = precondition(residual)
    image = curvature(precond)
    rz_now, wz_now = both_dots(residual, precond, image)
    alpha = rz_now / wz_now
    direction = precond
    along = image
    for iteration in range(ITERS):
        solution = solution + alpha * direction
        residual = residual - alpha * along
        if iteration + 1 < ITERS:
            precond = precondition(residual)
            image = curvature(precond)
            fresh, wz_now = both_dots(residual, precond, image)
            beta = fresh / rz_now
            alpha = fresh / (wz_now - beta * fresh / alpha)
            direction = precond + beta * direction
            along = image + beta * along
            rz_now = fresh
    return solution

def split_rows(row):
    top = row.astype(jnp.bfloat16).astype(jnp.float32)
    rest = row - top
    middle = rest.astype(jnp.bfloat16).astype(jnp.float32)
    bottom = rest - middle
    shape = (16, row.shape[1])
    line = lax.broadcasted_iota(jnp.int32, shape, 0)
    spread = lambda part: jnp.broadcast_to(part, shape)
    picked = jnp.where(
        line == 0,
        spread(top),
        jnp.where(line == 1, spread(middle), jnp.where(line == 2, spread(bottom), 0.0)),
    )
    return picked.astype(jnp.bfloat16)


def add_rows(parts):
    return parts[0:1] + parts[1:2] + parts[2:3]


def mxu(left, right, left_dim, right_dim):
    return lax.dot_general(
        left, right, (((left_dim,), (right_dim,)), ((), ())), preferred_element_type=jnp.float32
    )


def row_times(row, matrix):
    return add_rows(mxu(split_rows(row), matrix, 1, 0))


def row_times_transposed(row, matrix):
    return add_rows(mxu(split_rows(row), matrix, 1, 1))


def place():
    feat = lax.axis_index("feat")
    samp = lax.axis_index("samp")
    return feat // QUAD, feat % QUAD, samp


def greet(peers):
    barrier = pltpu.get_barrier_semaphore()
    for peer in peers:
        pl.semaphore_signal(barrier, inc=1, device_id=peer, device_id_type=MESH)
    return lambda: pl.semaphore_wait(barrier, len(peers))


def remote(source, target, send_sem, recv_sem, peer):
    return pltpu.make_async_remote_copy(
        src_ref=source,
        dst_ref=target,
        send_sem=send_sem,
        recv_sem=recv_sem,
        device_id=peer,
        device_id_type=MESH,
    )


def start_exchange(slots, mine, peers, send_sems, recv_sems):
    copies = []
    for number, peer in enumerate(peers):
        copy = remote(
            slots.at[mine], slots.at[mine], send_sems.at[number], recv_sems.at[number], peer
        )
        copy.start()
        copies.append(copy)
    return copies


def finish(copies):
    for copy in copies:
        copy.wait()


def total_of(slots, count):
    value = slots[0]
    for number in range(1, count):
        value = value + slots[number]
    return value


def quad_peers(depth, quarter, samp):
    return [{"feat": depth * QUAD + (quarter + k) % QUAD, "samp": samp} for k in range(1, QUAD)]


def depth_peers(layers, depth, quarter, samp):
    return [
        {"feat": ((depth + k) % layers) * QUAD + quarter, "samp": samp} for k in range(1, layers)
    ]


def plane_peers(depth, quarter, samp):
    member = samp * QUAD + quarter
    peers = []
    for k in range(1, 2 * QUAD):
        other = (member + k) % (2 * QUAD)
        peers.append({"feat": depth * QUAD + other % QUAD, "samp": other // QUAD})
    return peers


CHUNKS = 4


def gram_kernel(
    layers, features_home, weights, labels, sampled,
    scaled_home, gram_home, gradient, upper, lower, size,
    scaled, gram, inverse, pair, features, chosen, own_rows, sent_rows, came_rows, quad_slots, depth_slots, root_sent, root_came, grad_sent, grad_came,
    load_sem, store_sem, ship_send, ship_recv, quad_send, quad_recv, depth_send, depth_recv, small_send, small_recv,
):
    depth, quarter, samp = place()
    rows, columns = features.shape
    samples = sampled.shape[1]
    half = columns // 2
    partner = {"feat": depth * QUAD + quarter, "samp": 1 - samp}
    across = quad_peers(depth, quarter, samp)
    along = depth_peers(layers, depth, quarter, samp)
    mine_at = pl.multiple_of(samp * half, 128)
    other_at = pl.multiple_of((1 - samp) * half, 128)
    piece = samples // CHUNKS

    def load(number, start):
        return pltpu.make_async_copy(
            features_home.at[:, pl.ds(start, half)],
            features.at[:, pl.ds(start, half)],
            load_sem.at[number],
        )

    load_other, load_mine = load(0, other_at), load(1, mine_at)
    load_other.start()
    load_mine.start()
    wait_all = greet([partner] + across + along)
    names = jnp.transpose(jnp.broadcast_to(sampled[...], (128, samples)))

    def choose(first):
        wanted = names[first : first + piece]
        lane = lax.broadcasted_iota(jnp.int32, wanted.shape, 1)
        for start in range(0, rows, 128):
            hot = jnp.where(lane + start == wanted, 1.0, 0.0)
            chosen[first : first + piece, start : start + 128] = hot.astype(jnp.bfloat16)

    def ship(number):
        first = number * piece
        return remote(
            sent_rows.at[pl.ds(first, piece)],
            came_rows.at[pl.ds(first, piece)],
            ship_send.at[number],
            ship_recv.at[number],
            partner,
        )

    for number in range(CHUNKS):
        first = number * piece
        choose(first)
        if number == 0:
            load_other.wait()
        sent_rows[pl.ds(first, piece), :] = mxu(
            chosen[pl.ds(first, piece), :], features[:, pl.ds(other_at, half)], 1, 0
        ).astype(jnp.bfloat16)
        if number == 0:
            wait_all()
        ship(number).start()
    load_mine.wait()
    quad_slots[quarter] = row_times_transposed(weights[...], features[...])
    quad_copies = start_exchange(quad_slots, quarter, across, quad_send, quad_recv)

    def pick_own(number, carry):
        first = pl.multiple_of(number * piece, 128)
        own_rows[pl.ds(first, piece), :] = mxu(
            chosen[pl.ds(first, piece), :], features[:, pl.ds(mine_at, half)], 1, 0
        ).astype(jnp.bfloat16)
        return carry

    finish(quad_copies)
    depth_slots[depth] = total_of(quad_slots, QUAD)
    depth_copies = start_exchange(depth_slots, depth, along, depth_send, depth_recv)
    lax.fori_loop(0, CHUNKS, pick_own, 0)
    finish(depth_copies)
    margin = total_of(depth_slots, layers)
    probability = 1.0 / (1.0 + jnp.exp(-margin))
    root = jnp.sqrt(probability * (1.0 - probability))
    own_root = row_times_transposed(root, chosen[...])
    root_sent[...] = own_root
    root_copy = remote(root_sent, root_came, small_send.at[0], small_recv.at[0], partner)
    root_copy.start()
    residue = probability - labels[...].astype(jnp.float32)
    grad_sent[...] = row_times(residue, features[:, pl.ds(other_at, half)])
    grad_copy = remote(grad_sent, grad_came, small_send.at[1], small_recv.at[1], partner)
    grad_copy.start()
    own_grad = row_times(residue, features[:, pl.ds(mine_at, half)])

    def scale_into(source, factor, first, start):
        for column in range(0, half, 128):
            wide = source[pl.ds(first, piece), column : column + 128].astype(jnp.float32) * factor
            scaled[pl.ds(start, piece), column : column + 128] = wide.astype(jnp.bfloat16)

    def root_factor(root_row, number):
        part = root_row[:, number * piece : (number + 1) * piece]
        return jnp.transpose(jnp.broadcast_to(part, (128, piece)))

    mine_row = pl.multiple_of(samp * samples, 128)
    other_row = pl.multiple_of((1 - samp) * samples, 128)
    for number in range(CHUNKS):
        first = number * piece
        scale_into(own_rows, root_factor(own_root, number), first, mine_row + first)
    stores = [
        pltpu.make_async_copy(
            scaled.at[pl.ds(mine_row, samples)],
            scaled_home.at[pl.ds(mine_row, samples)],
            store_sem.at[CHUNKS],
        )
    ]
    stores[0].start()
    own_block = scaled[pl.ds(mine_row, samples), :]
    gram[...] = mxu(own_block, own_block, 0, 0)
    ridge_term = RIDGE_COEF / F
    shape = gram.shape
    same = lax.broadcasted_iota(jnp.int32, shape, 0) == lax.broadcasted_iota(jnp.int32, shape, 1)
    eye = jnp.where(same, 1.0, 0.0)
    bound = None
    for number in range(CHUNKS):
        first = number * piece
        if number == CHUNKS - 1:
            bound = early_inverse(gram[...] / (samples + first) + ridge_term * eye, eye, inverse, pair)
        ship(number).wait()
        if number == 0:
            root_copy.wait()
        scale_into(came_rows, root_factor(root_came[...], number), first, other_row + first)
        store = pltpu.make_async_copy(
            scaled.at[pl.ds(other_row + first, piece)],
            scaled_home.at[pl.ds(other_row + first, piece)],
            store_sem.at[number],
        )
        store.start()
        stores.append(store)
        block = scaled[pl.ds(other_row + first, piece), :]
        gram[...] += mxu(block, block, 0, 0)
    gram[...] = gram[...] / (2 * samples) + ridge_term * eye
    store = pltpu.make_async_copy(gram, gram_home, store_sem.at[CHUNKS + 1])
    store.start()
    stores.append(store)
    size[...] = jnp.broadcast_to(late_inverse(gram, bound, eye, inverse, pair, upper, lower), (1, 128))
    grad_copy.wait()
    gradient[...] = (own_grad + grad_came[...]) / (2 * rows) + ridge_term * weights[
        :, pl.ds(mine_at, half)
    ]
    for store in stores:
        store.wait()


SQUARINGS = 5
POLISH = 2
LIMIT = 60
DAMP = 0.6
SETTLED = 0.02


def halves(value):
    top = value.astype(jnp.bfloat16)
    return top, (value - top.astype(jnp.float32)).astype(jnp.bfloat16)


def raise_power(inverse, pair, count):
    order = inverse.shape[0]

    def square(_, carry):
        product = mxu(pair[...], pair[:order], 1, 0)
        value = inverse[...] + product[order:]
        inverse[...] = value
        pair[:order] = product[:order].astype(jnp.bfloat16)
        pair[order:] = value.astype(jnp.bfloat16)
        return carry

    lax.fori_loop(0, count - 1, square, 0)
    inverse[...] += mxu(pair[order:], pair[:order], 1, 0)


def early_inverse(early, eye, inverse, pair):
    order = early.shape[0]
    norm = lambda matrix: jnp.max(
        jnp.sum(jnp.abs(matrix), axis=0, keepdims=True), axis=1, keepdims=True
    )
    first_bound = norm(early)
    first = (early / first_bound).astype(jnp.bfloat16)
    squared = mxu(first, first, 1, 0)
    ratio = jnp.sqrt(norm(squared))
    bound = first_bound * ratio
    unit = early / bound
    value = 2.0 * eye - unit
    inverse[...] = value
    pair[:order] = (eye - 2.0 * unit + squared / (ratio * ratio)).astype(jnp.bfloat16)
    pair[order:] = value.astype(jnp.bfloat16)
    raise_power(inverse, pair, SQUARINGS)
    return bound


def late_inverse(gram, bound, eye, inverse, pair, upper, lower):
    order = gram.shape[0]
    unit_top, unit_low = halves(gram[...] / bound)
    value = DAMP * inverse[...]
    inverse[...] = value
    top = value.astype(jnp.bfloat16)
    pair[order:] = top
    pair[:order] = (eye - mxu(unit_top, top, 1, 0)).astype(jnp.bfloat16)
    raise_power(inverse, pair, 2)
    left = None
    for _ in range(POLISH):
        value = inverse[...]
        top, low = halves(value)
        product = mxu(unit_top, top, 1, 0) + mxu(unit_top, low, 1, 0) + mxu(unit_low, top, 1, 0)
        left = eye - product
        inverse[...] = value + mxu(top, left.astype(jnp.bfloat16), 1, 0)
    top, low = halves(inverse[...] / bound)
    upper[...] = top
    lower[...] = low
    return jnp.sum(jnp.sum(left * left, axis=0, keepdims=True), axis=1, keepdims=True)


def rescue_kernel(size, gram_home, _upper, _lower, upper_home, lower_home, unit, inverse, top_half, low_half):
    settled = size[0, 0] < SETTLED

    @pl.when(jnp.logical_not(settled))
    def _():
        pltpu.sync_copy(gram_home, unit)
        bound = jnp.max(jnp.sum(jnp.abs(unit[...]), axis=0, keepdims=True))
        unit[...] = unit[...] / bound
        shape = unit.shape
        eye = jnp.where(
            lax.broadcasted_iota(jnp.int32, shape, 0) == lax.broadcasted_iota(jnp.int32, shape, 1),
            1.0,
            0.0,
        )
        inverse[...] = eye

        def exact(left, right):
            return jnp.dot(
                left, right, precision=lax.Precision.HIGHEST, preferred_element_type=jnp.float32
            )

        def going(state):
            count, size_now = state
            return jnp.logical_and(count < LIMIT, size_now > 1e-8)

        def step(state):
            count, _ = state
            value = inverse[...]
            left = eye - exact(unit[...], value)
            fresh = value + exact(value, left)
            inverse[...] = 0.5 * (fresh + jnp.transpose(fresh))
            return count + 1, jnp.sum(left * left)

        lax.while_loop(going, step, (jnp.int32(0), jnp.float32(1.0)))
        top, low = halves(inverse[...] / bound)
        top_half[...] = top
        low_half[...] = low
        pltpu.sync_copy(top_half, upper_home)
        pltpu.sync_copy(low_half, lower_home)


def descent_kernel(
    layers, scaled_home, upper, lower, gradient,
    step,
    scaled, plane_slots, depth_slots, part_sent, part_came,
    load_sem, plane_send, plane_recv, depth_send, depth_recv, part_send, part_recv,
):
    depth, quarter, samp = place()
    samples, half = scaled.shape
    partner = {"feat": depth * QUAD + quarter, "samp": 1 - samp}
    plane = plane_peers(depth, quarter, samp)
    along = depth_peers(layers, depth, quarter, samp)
    load = pltpu.make_async_copy(scaled_home, scaled, load_sem.at[0])
    load.start()
    wait_all = greet(plane + along)
    member = samp * QUAD + quarter
    ridge_term = RIDGE_COEF / F
    lane = lax.broadcasted_iota(jnp.int32, (1, 128), 1)

    def precondition(vector):
        parts = split_rows(vector)
        return add_rows(mxu(parts, upper[...], 1, 0) + mxu(parts, lower[...], 1, 0))

    def total(row):
        return jnp.sum(row, axis=1, keepdims=True)

    residual = -gradient[...]
    answer = jnp.zeros_like(residual)
    direction = jnp.zeros_like(residual)
    twin_answer = jnp.zeros_like(residual)
    twin_direction = jnp.zeros_like(residual)
    along_rows = None
    rz_now = None
    length = None
    for iteration in range(ITERS):
        precond = precondition(residual)
        numbers = jnp.where(
            lane == 0,
            total(residual * precond),
            jnp.where(
                lane == 1,
                total(precond * precond),
                jnp.where(lane == 2, total(precond * direction), 0.0),
            ),
        )
        mine = plane_slots.at[iteration, member]
        part_sent[iteration] = precond
        if iteration == 0:
            load.wait()
        mine[:, :samples] = row_times_transposed(precond, scaled[...])
        mine[:, samples:] = numbers
        if iteration == 0:
            wait_all()
        plane_copies = start_exchange(
            plane_slots.at[iteration], member, plane, plane_send.at[iteration], plane_recv.at[iteration]
        )
        twin_copy = remote(
            part_sent.at[iteration],
            part_came.at[iteration],
            part_send.at[iteration],
            part_recv.at[iteration],
            partner,
        )
        twin_copy.start()
        finish(plane_copies)
        depth_slots[iteration, depth] = total_of(plane_slots.at[iteration], 2 * QUAD)
        finish(
            start_exchange(
                depth_slots.at[iteration], depth, along, depth_send.at[iteration], depth_recv.at[iteration]
            )
        )
        twin_copy.wait()
        twin_precond = part_came[iteration]
        summed = total_of(depth_slots.at[iteration], layers)
        image_rows = summed[:, :samples]
        fresh = summed[:, samples : samples + 1]
        square = summed[:, samples + 1 : samples + 2]
        cross = summed[:, samples + 2 : samples + 3]
        if iteration == 0:
            direction = precond
            twin_direction = twin_precond
            along_rows = image_rows
            length = square
        else:
            beta = fresh / rz_now
            direction = precond + beta * direction
            twin_direction = twin_precond + beta * twin_direction
            along_rows = image_rows + beta * along_rows
            length = square + 2.0 * beta * cross + beta * beta * length
        rz_now = fresh
        alpha = rz_now / (total(along_rows * along_rows) / samples + ridge_term * length)
        answer = answer + alpha * direction
        twin_answer = twin_answer + alpha * twin_direction
        if iteration + 1 < ITERS:
            image = row_times(along_rows, scaled[...]) / samples + ridge_term * direction
            residual = residual - alpha * image
    step[:, pl.ds(pl.multiple_of(samp * half, 128), half)] = answer
    step[:, pl.ds(pl.multiple_of((1 - samp) * half, 128), half)] = twin_answer


def split_device(features, labels, weights, sampled):
    rows, columns = features.shape
    samples = sampled.shape[0]
    half = columns // 2
    layers = lax.axis_size("feat") // QUAD
    shaped = jax.ShapeDtypeStruct
    whole = pl.BlockSpec(memory_space=pltpu.VMEM)
    dma = pltpu.SemaphoreType.DMA
    vmem = pltpu.VMEM
    anywhere = pl.BlockSpec(memory_space=pl.ANY)
    scaled, gram, gradient, upper, lower, size = pl.pallas_call(
        functools.partial(gram_kernel, layers),
        out_shape=(
            shaped((2 * samples, half), jnp.bfloat16),
            shaped((half, half), jnp.float32),
            shaped((1, half), jnp.float32),
            shaped((half, half), jnp.bfloat16),
            shaped((half, half), jnp.bfloat16),
            shaped((1, 128), jnp.float32),
        ),
        in_specs=[anywhere] + [whole] * 3,
        out_specs=(anywhere,) * 2 + (whole,) * 4,
        scratch_shapes=[
            vmem((2 * samples, half), jnp.bfloat16),
            vmem((half, half), jnp.float32),
            vmem((half, half), jnp.float32),
            vmem((2 * half, half), jnp.bfloat16),
            vmem((rows, columns), jnp.bfloat16),
            vmem((samples, rows), jnp.bfloat16),
            vmem((samples, half), jnp.bfloat16),
            vmem((samples, half), jnp.bfloat16),
            vmem((samples, half), jnp.bfloat16),
            vmem((QUAD, 1, rows), jnp.float32),
            vmem((layers, 1, rows), jnp.float32),
            vmem((1, samples), jnp.float32),
            vmem((1, samples), jnp.float32),
            vmem((1, half), jnp.float32),
            vmem((1, half), jnp.float32),
            dma((2,)),
            dma((CHUNKS + 2,)),
            dma((CHUNKS,)),
            dma((CHUNKS,)),
            dma((QUAD - 1,)),
            dma((QUAD - 1,)),
            dma((layers - 1,)),
            dma((layers - 1,)),
            dma((2,)),
            dma((2,)),
        ],
        compiler_params=pltpu.CompilerParams(collective_id=0, has_side_effects=True),
    )(features, weights[None, :], labels[None, :], sampled[None, :])
    upper, lower = pl.pallas_call(
        rescue_kernel,
        out_shape=(shaped((half, half), jnp.bfloat16),) * 2,
        in_specs=[pl.BlockSpec(memory_space=pltpu.SMEM)] + [anywhere] * 3,
        out_specs=(anywhere,) * 2,
        scratch_shapes=[
            vmem((half, half), jnp.float32),
            vmem((half, half), jnp.float32),
            vmem((half, half), jnp.bfloat16),
            vmem((half, half), jnp.bfloat16),
        ],
        input_output_aliases={2: 0, 3: 1},
    )(size, gram, upper, lower)
    width = 2 * samples + 128
    step = pl.pallas_call(
        functools.partial(descent_kernel, layers),
        out_shape=shaped((1, columns), jnp.float32),
        in_specs=[anywhere] + [whole] * 3,
        out_specs=whole,
        scratch_shapes=[
            vmem((2 * samples, half), jnp.bfloat16),
            vmem((ITERS, 2 * QUAD, 1, width), jnp.float32),
            vmem((ITERS, layers, 1, width), jnp.float32),
            vmem((ITERS, 1, half), jnp.float32),
            vmem((ITERS, 1, half), jnp.float32),
            dma((1,)),
            dma((ITERS, 2 * QUAD - 1)),
            dma((ITERS, 2 * QUAD - 1)),
            dma((ITERS, layers - 1)),
            dma((ITERS, layers - 1)),
            dma((ITERS,)),
            dma((ITERS,)),
        ],
        compiler_params=pltpu.CompilerParams(collective_id=1, has_side_effects=True),
    )(scaled, upper, lower, gradient)
    return step[0]


def solution(mesh):
    placed = (P("samp", "feat"), P("samp"), P("feat"), P("samp"))
    devices, groups = mesh.shape["feat"], mesh.shape["samp"]
    apart = groups == 2 and devices % QUAD == 0 and devices > QUAD and F // devices == 2 * BLK
    return jax.shard_map(
        split_device if apart else per_device,
        mesh=mesh,
        in_specs=placed,
        out_specs=P("feat"),
        check_vma=False,
    )
```

```python
import functools

import jax
import jax.numpy as jnp
from jax import lax
from jax.experimental import pallas as pl
from jax.experimental.pallas import tpu as pltpu
from jax.sharding import PartitionSpec as P

F = 16384
BLK = 512
ITERS = 3
QUAD = 4
MESH = pl.DeviceIdType.MESH


RIDGE_COEF = 0.05


def partner_2(value, axis, apart):
    mask = 2**apart
    pairs = [(source, source ^ mask) for source in range(lax.axis_size(axis))]
    return lax.ppermute(value, axis, pairs)


def split_parts(vector):
    upper_part = vector.astype(jnp.bfloat16)
    widened = lax.optimization_barrier(upper_part).astype(jnp.float32)
    lower_part = (vector - widened).astype(jnp.bfloat16)
    return (upper_part, lower_part)


def matrix_vector(matrix, vector):
    upper_part, lower_part = split_parts(vector)
    return jnp.dot(matrix, upper_part, preferred_element_type=jnp.float32) + jnp.dot(
        matrix, lower_part, preferred_element_type=jnp.float32
    )


def vector_matrix(vector, matrix):
    upper_part, lower_part = split_parts(vector)
    return jnp.dot(upper_part, matrix, preferred_element_type=jnp.float32) + jnp.dot(
        lower_part, matrix, preferred_element_type=jnp.float32
    )


def block_solve(factors, rhs_blocks):
    forward = jax.vmap(
        lambda factor, column: jax.scipy.linalg.solve_triangular(factor, column, lower=True)
    )(factors, rhs_blocks)
    return jax.vmap(
        lambda factor, column: jax.scipy.linalg.solve_triangular(
            factor, column, lower=True, trans=1
        )
    )(factors, forward)


def local_blocks(scaled):
    blocks = scaled.reshape(scaled.shape[0], scaled.shape[1] // BLK, BLK)
    return jnp.einsum("hkb,hkc->kbc", blocks, blocks, preferred_element_type=jnp.float32)


def per_device(features, labels, weights, sampled):
    columns = features.shape[1]
    sample_rows = sampled.shape[0]
    groups = lax.axis_size("samp")
    row_total = features.shape[0] * groups
    hess_total = sample_rows * groups
    ridge_term = RIDGE_COEF / F
    paired = columns < BLK
    upper_side = lax.axis_index("feat") % 2 == 1
    margin = lax.psum(matrix_vector(features, weights), "feat")
    probability = jax.nn.sigmoid(margin)
    residue = probability - labels.astype(jnp.float32)
    gradient = lax.psum(vector_matrix(residue, features), "samp") / row_total + ridge_term * weights
    chosen = jnp.take(probability, sampled)
    root_curv = jnp.sqrt(chosen * (1.0 - chosen))
    scaled = (jnp.take(features, sampled, axis=0) * root_curv[:, None]).astype(jnp.bfloat16)
    if paired:
        partner = partner_2(scaled, "feat", 0)
        joined = jnp.where(
            upper_side, jnp.concatenate([partner, scaled], 1), jnp.concatenate([scaled, partner], 1)
        )
        partial_gram = jnp.einsum("hb,hc->bc", joined, joined, preferred_element_type=jnp.float32)[
            None
        ]
    else:
        partial_gram = local_blocks(scaled)
    summed = lax.psum(partial_gram, "samp")
    gram = summed / hess_total + ridge_term * jnp.eye(BLK, dtype=jnp.float32)
    factors = jnp.linalg.cholesky(gram)

    def precondition(vector):
        if paired:
            other = partner_2(vector, "feat", 0)
            joined_vec = jnp.where(
                upper_side, jnp.concatenate([other, vector]), jnp.concatenate([vector, other])
            )[None]
            solved = block_solve(factors, joined_vec)[0]
            return jnp.where(upper_side, solved[columns:], solved[:columns])
        return block_solve(factors, vector.reshape(-1, BLK)).reshape(columns)

    def curvature(vector):
        image_rows = lax.psum(matrix_vector(scaled, vector), "feat")
        back = lax.psum(vector_matrix(image_rows, scaled), "samp")
        return back / hess_total + ridge_term * vector

    solution = jnp.zeros((columns,), jnp.float32)
    residual = -gradient

    def both_dots(resid_vec, precond_vec, image_vec):
        return lax.psum(
            (jnp.sum(resid_vec * precond_vec), jnp.sum(image_vec * precond_vec)), "feat"
        )

    precond = precondition(residual)
    image = curvature(precond)
    rz_now, wz_now = both_dots(residual, precond, image)
    alpha = rz_now / wz_now
    direction = precond
    along = image
    for iteration in range(ITERS):
        solution = solution + alpha * direction
        residual = residual - alpha * along
        if iteration + 1 < ITERS:
            precond = precondition(residual)
            image = curvature(precond)
            fresh, wz_now = both_dots(residual, precond, image)
            beta = fresh / rz_now
            alpha = fresh / (wz_now - beta * fresh / alpha)
            direction = precond + beta * direction
            along = image + beta * along
            rz_now = fresh
    return solution

def split_rows(row):
    top = row.astype(jnp.bfloat16).astype(jnp.float32)
    rest = row - top
    middle = rest.astype(jnp.bfloat16).astype(jnp.float32)
    bottom = rest - middle
    shape = (16, row.shape[1])
    line = lax.broadcasted_iota(jnp.int32, shape, 0)
    spread = lambda part: jnp.broadcast_to(part, shape)
    picked = jnp.where(
        line == 0,
        spread(top),
        jnp.where(line == 1, spread(middle), jnp.where(line == 2, spread(bottom), 0.0)),
    )
    return picked.astype(jnp.bfloat16)


def add_rows(parts):
    return parts[0:1] + parts[1:2] + parts[2:3]


def mxu(left, right, left_dim, right_dim):
    return lax.dot_general(
        left, right, (((left_dim,), (right_dim,)), ((), ())), preferred_element_type=jnp.float32
    )


def row_times(row, matrix):
    return add_rows(mxu(split_rows(row), matrix, 1, 0))


def row_times_transposed(row, matrix):
    return add_rows(mxu(split_rows(row), matrix, 1, 1))


def place():
    feat = lax.axis_index("feat")
    samp = lax.axis_index("samp")
    return feat // QUAD, feat % QUAD, samp


def greet(peers):
    barrier = pltpu.get_barrier_semaphore()
    for peer in peers:
        pl.semaphore_signal(barrier, inc=1, device_id=peer, device_id_type=MESH)
    return lambda: pl.semaphore_wait(barrier, len(peers))


def remote(source, target, send_sem, recv_sem, peer):
    return pltpu.make_async_remote_copy(
        src_ref=source,
        dst_ref=target,
        send_sem=send_sem,
        recv_sem=recv_sem,
        device_id=peer,
        device_id_type=MESH,
    )


def start_exchange(slots, mine, peers, send_sems, recv_sems):
    copies = []
    for number, peer in enumerate(peers):
        copy = remote(
            slots.at[mine], slots.at[mine], send_sems.at[number], recv_sems.at[number], peer
        )
        copy.start()
        copies.append(copy)
    return copies


def finish(copies):
    for copy in copies:
        copy.wait()


def total_of(slots, count):
    value = slots[0]
    for number in range(1, count):
        value = value + slots[number]
    return value


def quad_peers(depth, quarter, samp):
    return [{"feat": depth * QUAD + (quarter + k) % QUAD, "samp": samp} for k in range(1, QUAD)]


def depth_peers(layers, depth, quarter, samp):
    return [
        {"feat": ((depth + k) % layers) * QUAD + quarter, "samp": samp} for k in range(1, layers)
    ]


def plane_peers(depth, quarter, samp):
    member = samp * QUAD + quarter
    peers = []
    for k in range(1, 2 * QUAD):
        other = (member + k) % (2 * QUAD)
        peers.append({"feat": depth * QUAD + other % QUAD, "samp": other // QUAD})
    return peers


CHUNKS = 4
AHEAD = 2


def gram_kernel(
    layers, features_home, weights, labels, sampled,
    scaled_home, gram_home, gradient, upper, lower, size,
    scaled, gram, inverse, pair, features, chosen, own_rows, sent_rows, came_rows, quad_slots, depth_slots, root_sent, root_came, grad_sent, grad_came,
    load_sem, store_sem, ship_send, ship_recv, quad_send, quad_recv, depth_send, depth_recv, small_send, small_recv,
):
    depth, quarter, samp = place()
    rows, columns = features.shape
    samples = sampled.shape[1]
    half = columns // 2
    partner = {"feat": depth * QUAD + quarter, "samp": 1 - samp}
    across = quad_peers(depth, quarter, samp)
    along = depth_peers(layers, depth, quarter, samp)
    mine_at = pl.multiple_of(samp * half, 128)
    other_at = pl.multiple_of((1 - samp) * half, 128)
    piece = samples // CHUNKS

    def load(number, start):
        return pltpu.make_async_copy(
            features_home.at[:, pl.ds(start, half)],
            features.at[:, pl.ds(start, half)],
            load_sem.at[number],
        )

    load_other, load_mine = load(0, other_at), load(1, mine_at)
    load_other.start()
    load_mine.start()
    wait_all = greet([partner] + across + along)
    names = jnp.transpose(jnp.broadcast_to(sampled[...], (128, samples)))

    def choose(first):
        wanted = names[first : first + piece]
        lane = lax.broadcasted_iota(jnp.int32, wanted.shape, 1)
        for start in range(0, rows, 128):
            hot = jnp.where(lane + start == wanted, 1.0, 0.0)
            chosen[first : first + piece, start : start + 128] = hot.astype(jnp.bfloat16)

    def ship(number):
        first = number * piece
        return remote(
            sent_rows.at[pl.ds(first, piece)],
            came_rows.at[pl.ds(first, piece)],
            ship_send.at[number],
            ship_recv.at[number],
            partner,
        )

    for number in range(CHUNKS):
        first = number * piece
        choose(first)
        if number == 0:
            load_other.wait()
        sent_rows[pl.ds(first, piece), :] = mxu(
            chosen[pl.ds(first, piece), :], features[:, pl.ds(other_at, half)], 1, 0
        ).astype(jnp.bfloat16)
        if number == 0:
            wait_all()
        if number < AHEAD:
            ship(number).start()
    load_mine.wait()
    quad_slots[quarter] = row_times_transposed(weights[...], features[...])
    quad_copies = start_exchange(quad_slots, quarter, across, quad_send, quad_recv)

    def pick_own(number, carry):
        first = pl.multiple_of(number * piece, 128)
        own_rows[pl.ds(first, piece), :] = mxu(
            chosen[pl.ds(first, piece), :], features[:, pl.ds(mine_at, half)], 1, 0
        ).astype(jnp.bfloat16)
        return carry

    finish(quad_copies)
    depth_slots[depth] = total_of(quad_slots, QUAD)
    depth_copies = start_exchange(depth_slots, depth, along, depth_send, depth_recv)
    lax.fori_loop(0, CHUNKS, pick_own, 0)
    finish(depth_copies)
    margin = total_of(depth_slots, layers)
    probability = 1.0 / (1.0 + jnp.exp(-margin))
    root = jnp.sqrt(probability * (1.0 - probability))
    own_root = row_times_transposed(root, chosen[...])
    root_sent[...] = own_root
    root_copy = remote(root_sent, root_came, small_send.at[0], small_recv.at[0], partner)
    root_copy.start()
    for number in range(AHEAD, CHUNKS):
        ship(number).start()
    residue = probability - labels[...].astype(jnp.float32)
    grad_sent[...] = row_times(residue, features[:, pl.ds(other_at, half)])
    grad_copy = remote(grad_sent, grad_came, small_send.at[1], small_recv.at[1], partner)
    grad_copy.start()
    own_grad = row_times(residue, features[:, pl.ds(mine_at, half)])

    def scale_into(source, factor, first, start):
        for column in range(0, half, 128):
            wide = source[pl.ds(first, piece), column : column + 128].astype(jnp.float32) * factor
            scaled[pl.ds(start, piece), column : column + 128] = wide.astype(jnp.bfloat16)

    def root_factor(root_row, number):
        part = root_row[:, number * piece : (number + 1) * piece]
        return jnp.transpose(jnp.broadcast_to(part, (128, piece)))

    mine_row = pl.multiple_of(samp * samples, 128)
    other_row = pl.multiple_of((1 - samp) * samples, 128)
    for number in range(CHUNKS):
        first = number * piece
        scale_into(own_rows, root_factor(own_root, number), first, mine_row + first)
    stores = [
        pltpu.make_async_copy(
            scaled.at[pl.ds(mine_row, samples)],
            scaled_home.at[pl.ds(mine_row, samples)],
            store_sem.at[CHUNKS],
        )
    ]
    stores[0].start()
    own_block = scaled[pl.ds(mine_row, samples), :]
    gram[...] = mxu(own_block, own_block, 0, 0)
    ridge_term = RIDGE_COEF / F
    shape = gram.shape
    same = lax.broadcasted_iota(jnp.int32, shape, 0) == lax.broadcasted_iota(jnp.int32, shape, 1)
    eye = jnp.where(same, 1.0, 0.0)
    bound = None
    for number in range(CHUNKS):
        first = number * piece
        if number == CHUNKS - 1:
            bound = early_inverse(gram[...] / (samples + first) + ridge_term * eye, eye, inverse, pair)
        ship(number).wait()
        if number == 0:
            root_copy.wait()
        scale_into(came_rows, root_factor(root_came[...], number), first, other_row + first)
        store = pltpu.make_async_copy(
            scaled.at[pl.ds(other_row + first, piece)],
            scaled_home.at[pl.ds(other_row + first, piece)],
            store_sem.at[number],
        )
        store.start()
        stores.append(store)
        block = scaled[pl.ds(other_row + first, piece), :]
        gram[...] += mxu(block, block, 0, 0)
    gram[...] = gram[...] / (2 * samples) + ridge_term * eye
    store = pltpu.make_async_copy(gram, gram_home, store_sem.at[CHUNKS + 1])
    store.start()
    stores.append(store)
    size[...] = jnp.broadcast_to(late_inverse(gram, bound, eye, inverse, pair, upper, lower), (1, 128))
    grad_copy.wait()
    gradient[...] = (own_grad + grad_came[...]) / (2 * rows) + ridge_term * weights[
        :, pl.ds(mine_at, half)
    ]
    for store in stores:
        store.wait()


SQUARINGS = 5
POLISH = 2
LIMIT = 60
DAMP = 0.6
SETTLED = 0.02


def halves(value):
    top = value.astype(jnp.bfloat16)
    return top, (value - top.astype(jnp.float32)).astype(jnp.bfloat16)


def raise_power(inverse, pair, count):
    order = inverse.shape[0]

    def square(_, carry):
        product = mxu(pair[...], pair[:order], 1, 0)
        value = inverse[...] + product[order:]
        inverse[...] = value
        pair[:order] = product[:order].astype(jnp.bfloat16)
        pair[order:] = value.astype(jnp.bfloat16)
        return carry

    lax.fori_loop(0, count - 1, square, 0)
    inverse[...] += mxu(pair[order:], pair[:order], 1, 0)


def early_inverse(early, eye, inverse, pair):
    order = early.shape[0]
    norm = lambda matrix: jnp.max(
        jnp.sum(jnp.abs(matrix), axis=0, keepdims=True), axis=1, keepdims=True
    )
    first_bound = norm(early)
    first = (early / first_bound).astype(jnp.bfloat16)
    squared = mxu(first, first, 1, 0)
    ratio = jnp.sqrt(norm(squared))
    bound = first_bound * ratio
    unit = early / bound
    value = 2.0 * eye - unit
    inverse[...] = value
    pair[:order] = (eye - 2.0 * unit + squared / (ratio * ratio)).astype(jnp.bfloat16)
    pair[order:] = value.astype(jnp.bfloat16)
    raise_power(inverse, pair, SQUARINGS)
    return bound


def late_inverse(gram, bound, eye, inverse, pair, upper, lower):
    order = gram.shape[0]
    unit_top, unit_low = halves(gram[...] / bound)
    value = DAMP * inverse[...]
    inverse[...] = value
    top = value.astype(jnp.bfloat16)
    pair[order:] = top
    pair[:order] = (eye - mxu(unit_top, top, 1, 0)).astype(jnp.bfloat16)
    raise_power(inverse, pair, 2)
    left = None
    for _ in range(POLISH):
        value = inverse[...]
        top, low = halves(value)
        product = mxu(unit_top, top, 1, 0) + mxu(unit_top, low, 1, 0) + mxu(unit_low, top, 1, 0)
        left = eye - product
        inverse[...] = value + mxu(top, left.astype(jnp.bfloat16), 1, 0)
    top, low = halves(inverse[...] / bound)
    upper[...] = top
    lower[...] = low
    return jnp.sum(jnp.sum(left * left, axis=0, keepdims=True), axis=1, keepdims=True)


def rescue_kernel(size, gram_home, _upper, _lower, upper_home, lower_home, unit, inverse, top_half, low_half):
    settled = size[0, 0] < SETTLED

    @pl.when(jnp.logical_not(settled))
    def _():
        pltpu.sync_copy(gram_home, unit)
        bound = jnp.max(jnp.sum(jnp.abs(unit[...]), axis=0, keepdims=True))
        unit[...] = unit[...] / bound
        shape = unit.shape
        eye = jnp.where(
            lax.broadcasted_iota(jnp.int32, shape, 0) == lax.broadcasted_iota(jnp.int32, shape, 1),
            1.0,
            0.0,
        )
        inverse[...] = eye

        def exact(left, right):
            return jnp.dot(
                left, right, precision=lax.Precision.HIGHEST, preferred_element_type=jnp.float32
            )

        def going(state):
            count, size_now = state
            return jnp.logical_and(count < LIMIT, size_now > 1e-8)

        def step(state):
            count, _ = state
            value = inverse[...]
            left = eye - exact(unit[...], value)
            fresh = value + exact(value, left)
            inverse[...] = 0.5 * (fresh + jnp.transpose(fresh))
            return count + 1, jnp.sum(left * left)

        lax.while_loop(going, step, (jnp.int32(0), jnp.float32(1.0)))
        top, low = halves(inverse[...] / bound)
        top_half[...] = top
        low_half[...] = low
        pltpu.sync_copy(top_half, upper_home)
        pltpu.sync_copy(low_half, lower_home)


def descent_kernel(
    layers, scaled_home, upper, lower, gradient,
    step,
    scaled, plane_slots, depth_slots, part_sent, part_came,
    load_sem, plane_send, plane_recv, depth_send, depth_recv, part_send, part_recv,
):
    depth, quarter, samp = place()
    samples, half = scaled.shape
    partner = {"feat": depth * QUAD + quarter, "samp": 1 - samp}
    plane = plane_peers(depth, quarter, samp)
    along = depth_peers(layers, depth, quarter, samp)
    load = pltpu.make_async_copy(scaled_home, scaled, load_sem.at[0])
    load.start()
    wait_all = greet(plane + along)
    member = samp * QUAD + quarter
    ridge_term = RIDGE_COEF / F
    lane = lax.broadcasted_iota(jnp.int32, (1, 128), 1)

    def precondition(vector):
        parts = split_rows(vector)
        return add_rows(mxu(parts, upper[...], 1, 0) + mxu(parts, lower[...], 1, 0))

    def total(row):
        return jnp.sum(row, axis=1, keepdims=True)

    residual = -gradient[...]
    answer = jnp.zeros_like(residual)
    direction = jnp.zeros_like(residual)
    twin_answer = jnp.zeros_like(residual)
    twin_direction = jnp.zeros_like(residual)
    along_rows = None
    rz_now = None
    length = None
    for iteration in range(ITERS):
        precond = precondition(residual)
        numbers = jnp.where(
            lane == 0,
            total(residual * precond),
            jnp.where(
                lane == 1,
                total(precond * precond),
                jnp.where(lane == 2, total(precond * direction), 0.0),
            ),
        )
        mine = plane_slots.at[iteration, member]
        part_sent[iteration] = precond
        if iteration == 0:
            load.wait()
        mine[:, :samples] = row_times_transposed(precond, scaled[...])
        mine[:, samples:] = numbers
        if iteration == 0:
            wait_all()
        plane_copies = start_exchange(
            plane_slots.at[iteration], member, plane, plane_send.at[iteration], plane_recv.at[iteration]
        )
        twin_copy = remote(
            part_sent.at[iteration],
            part_came.at[iteration],
            part_send.at[iteration],
            part_recv.at[iteration],
            partner,
        )
        twin_copy.start()
        finish(plane_copies)
        depth_slots[iteration, depth] = total_of(plane_slots.at[iteration], 2 * QUAD)
        finish(
            start_exchange(
                depth_slots.at[iteration], depth, along, depth_send.at[iteration], depth_recv.at[iteration]
            )
        )
        twin_copy.wait()
        twin_precond = part_came[iteration]
        summed = total_of(depth_slots.at[iteration], layers)
        image_rows = summed[:, :samples]
        fresh = summed[:, samples : samples + 1]
        square = summed[:, samples + 1 : samples + 2]
        cross = summed[:, samples + 2 : samples + 3]
        if iteration == 0:
            direction = precond
            twin_direction = twin_precond
            along_rows = image_rows
            length = square
        else:
            beta = fresh / rz_now
            direction = precond + beta * direction
            twin_direction = twin_precond + beta * twin_direction
            along_rows = image_rows + beta * along_rows
            length = square + 2.0 * beta * cross + beta * beta * length
        rz_now = fresh
        alpha = rz_now / (total(along_rows * along_rows) / samples + ridge_term * length)
        answer = answer + alpha * direction
        twin_answer = twin_answer + alpha * twin_direction
        if iteration + 1 < ITERS:
            image = row_times(along_rows, scaled[...]) / samples + ridge_term * direction
            residual = residual - alpha * image
    step[:, pl.ds(pl.multiple_of(samp * half, 128), half)] = answer
    step[:, pl.ds(pl.multiple_of((1 - samp) * half, 128), half)] = twin_answer


def split_device(features, labels, weights, sampled):
    rows, columns = features.shape
    samples = sampled.shape[0]
    half = columns // 2
    layers = lax.axis_size("feat") // QUAD
    shaped = jax.ShapeDtypeStruct
    whole = pl.BlockSpec(memory_space=pltpu.VMEM)
    dma = pltpu.SemaphoreType.DMA
    vmem = pltpu.VMEM
    anywhere = pl.BlockSpec(memory_space=pl.ANY)
    scaled, gram, gradient, upper, lower, size = pl.pallas_call(
        functools.partial(gram_kernel, layers),
        out_shape=(
            shaped((2 * samples, half), jnp.bfloat16),
            shaped((half, half), jnp.float32),
            shaped((1, half), jnp.float32),
            shaped((half, half), jnp.bfloat16),
            shaped((half, half), jnp.bfloat16),
            shaped((1, 128), jnp.float32),
        ),
        in_specs=[anywhere] + [whole] * 3,
        out_specs=(anywhere,) * 2 + (whole,) * 4,
        scratch_shapes=[
            vmem((2 * samples, half), jnp.bfloat16),
            vmem((half, half), jnp.float32),
            vmem((half, half), jnp.float32),
            vmem((2 * half, half), jnp.bfloat16),
            vmem((rows, columns), jnp.bfloat16),
            vmem((samples, rows), jnp.bfloat16),
            vmem((samples, half), jnp.bfloat16),
            vmem((samples, half), jnp.bfloat16),
            vmem((samples, half), jnp.bfloat16),
            vmem((QUAD, 1, rows), jnp.float32),
            vmem((layers, 1, rows), jnp.float32),
            vmem((1, samples), jnp.float32),
            vmem((1, samples), jnp.float32),
            vmem((1, half), jnp.float32),
            vmem((1, half), jnp.float32),
            dma((2,)),
            dma((CHUNKS + 2,)),
            dma((CHUNKS,)),
            dma((CHUNKS,)),
            dma((QUAD - 1,)),
            dma((QUAD - 1,)),
            dma((layers - 1,)),
            dma((layers - 1,)),
            dma((2,)),
            dma((2,)),
        ],
        compiler_params=pltpu.CompilerParams(collective_id=0, has_side_effects=True),
    )(features, weights[None, :], labels[None, :], sampled[None, :])
    upper, lower = pl.pallas_call(
        rescue_kernel,
        out_shape=(shaped((half, half), jnp.bfloat16),) * 2,
        in_specs=[pl.BlockSpec(memory_space=pltpu.SMEM)] + [anywhere] * 3,
        out_specs=(anywhere,) * 2,
        scratch_shapes=[
            vmem((half, half), jnp.float32),
            vmem((half, half), jnp.float32),
            vmem((half, half), jnp.bfloat16),
            vmem((half, half), jnp.bfloat16),
        ],
        input_output_aliases={2: 0, 3: 1},
    )(size, gram, upper, lower)
    width = 2 * samples + 128
    step = pl.pallas_call(
        functools.partial(descent_kernel, layers),
        out_shape=shaped((1, columns), jnp.float32),
        in_specs=[anywhere] + [whole] * 3,
        out_specs=whole,
        scratch_shapes=[
            vmem((2 * samples, half), jnp.bfloat16),
            vmem((ITERS, 2 * QUAD, 1, width), jnp.float32),
            vmem((ITERS, layers, 1, width), jnp.float32),
            vmem((ITERS, 1, half), jnp.float32),
            vmem((ITERS, 1, half), jnp.float32),
            dma((1,)),
            dma((ITERS, 2 * QUAD - 1)),
            dma((ITERS, 2 * QUAD - 1)),
            dma((ITERS, layers - 1)),
            dma((ITERS, layers - 1)),
            dma((ITERS,)),
            dma((ITERS,)),
        ],
        compiler_params=pltpu.CompilerParams(collective_id=1, has_side_effects=True),
    )(scaled, upper, lower, gradient)
    return step[0]


def solution(mesh):
    placed = (P("samp", "feat"), P("samp"), P("feat"), P("samp"))
    devices, groups = mesh.shape["feat"], mesh.shape["samp"]
    apart = groups == 2 and devices % QUAD == 0 and devices > QUAD and F // devices == 2 * BLK
    return jax.shard_map(
        split_device if apart else per_device,
        mesh=mesh,
        in_specs=placed,
        out_specs=P("feat"),
        check_vma=False,
    )
```

```python
import functools

import jax
import jax.numpy as jnp
from jax import lax
from jax.experimental import pallas as pl
from jax.experimental.pallas import tpu as pltpu
from jax.sharding import PartitionSpec as P

F = 16384
BLK = 512
ITERS = 3
QUAD = 4
MESH = pl.DeviceIdType.MESH


RIDGE_COEF = 0.05


def partner_2(value, axis, apart):
    mask = 2**apart
    pairs = [(source, source ^ mask) for source in range(lax.axis_size(axis))]
    return lax.ppermute(value, axis, pairs)


def split_parts(vector):
    upper_part = vector.astype(jnp.bfloat16)
    widened = lax.optimization_barrier(upper_part).astype(jnp.float32)
    lower_part = (vector - widened).astype(jnp.bfloat16)
    return (upper_part, lower_part)


def matrix_vector(matrix, vector):
    upper_part, lower_part = split_parts(vector)
    return jnp.dot(matrix, upper_part, preferred_element_type=jnp.float32) + jnp.dot(
        matrix, lower_part, preferred_element_type=jnp.float32
    )


def vector_matrix(vector, matrix):
    upper_part, lower_part = split_parts(vector)
    return jnp.dot(upper_part, matrix, preferred_element_type=jnp.float32) + jnp.dot(
        lower_part, matrix, preferred_element_type=jnp.float32
    )


def block_solve(factors, rhs_blocks):
    forward = jax.vmap(
        lambda factor, column: jax.scipy.linalg.solve_triangular(factor, column, lower=True)
    )(factors, rhs_blocks)
    return jax.vmap(
        lambda factor, column: jax.scipy.linalg.solve_triangular(
            factor, column, lower=True, trans=1
        )
    )(factors, forward)


def local_blocks(scaled):
    blocks = scaled.reshape(scaled.shape[0], scaled.shape[1] // BLK, BLK)
    return jnp.einsum("hkb,hkc->kbc", blocks, blocks, preferred_element_type=jnp.float32)


def per_device(features, labels, weights, sampled):
    columns = features.shape[1]
    sample_rows = sampled.shape[0]
    groups = lax.axis_size("samp")
    row_total = features.shape[0] * groups
    hess_total = sample_rows * groups
    ridge_term = RIDGE_COEF / F
    paired = columns < BLK
    upper_side = lax.axis_index("feat") % 2 == 1
    margin = lax.psum(matrix_vector(features, weights), "feat")
    probability = jax.nn.sigmoid(margin)
    residue = probability - labels.astype(jnp.float32)
    gradient = lax.psum(vector_matrix(residue, features), "samp") / row_total + ridge_term * weights
    chosen = jnp.take(probability, sampled)
    root_curv = jnp.sqrt(chosen * (1.0 - chosen))
    scaled = (jnp.take(features, sampled, axis=0) * root_curv[:, None]).astype(jnp.bfloat16)
    if paired:
        partner = partner_2(scaled, "feat", 0)
        joined = jnp.where(
            upper_side, jnp.concatenate([partner, scaled], 1), jnp.concatenate([scaled, partner], 1)
        )
        partial_gram = jnp.einsum("hb,hc->bc", joined, joined, preferred_element_type=jnp.float32)[
            None
        ]
    else:
        partial_gram = local_blocks(scaled)
    summed = lax.psum(partial_gram, "samp")
    gram = summed / hess_total + ridge_term * jnp.eye(BLK, dtype=jnp.float32)
    factors = jnp.linalg.cholesky(gram)

    def precondition(vector):
        if paired:
            other = partner_2(vector, "feat", 0)
            joined_vec = jnp.where(
                upper_side, jnp.concatenate([other, vector]), jnp.concatenate([vector, other])
            )[None]
            solved = block_solve(factors, joined_vec)[0]
            return jnp.where(upper_side, solved[columns:], solved[:columns])
        return block_solve(factors, vector.reshape(-1, BLK)).reshape(columns)

    def curvature(vector):
        image_rows = lax.psum(matrix_vector(scaled, vector), "feat")
        back = lax.psum(vector_matrix(image_rows, scaled), "samp")
        return back / hess_total + ridge_term * vector

    solution = jnp.zeros((columns,), jnp.float32)
    residual = -gradient

    def both_dots(resid_vec, precond_vec, image_vec):
        return lax.psum(
            (jnp.sum(resid_vec * precond_vec), jnp.sum(image_vec * precond_vec)), "feat"
        )

    precond = precondition(residual)
    image = curvature(precond)
    rz_now, wz_now = both_dots(residual, precond, image)
    alpha = rz_now / wz_now
    direction = precond
    along = image
    for iteration in range(ITERS):
        solution = solution + alpha * direction
        residual = residual - alpha * along
        if iteration + 1 < ITERS:
            precond = precondition(residual)
            image = curvature(precond)
            fresh, wz_now = both_dots(residual, precond, image)
            beta = fresh / rz_now
            alpha = fresh / (wz_now - beta * fresh / alpha)
            direction = precond + beta * direction
            along = image + beta * along
            rz_now = fresh
    return solution

def split_rows(row):
    top = row.astype(jnp.bfloat16).astype(jnp.float32)
    rest = row - top
    middle = rest.astype(jnp.bfloat16).astype(jnp.float32)
    bottom = rest - middle
    shape = (16, row.shape[1])
    line = lax.broadcasted_iota(jnp.int32, shape, 0)
    spread = lambda part: jnp.broadcast_to(part, shape)
    picked = jnp.where(
        line == 0,
        spread(top),
        jnp.where(line == 1, spread(middle), jnp.where(line == 2, spread(bottom), 0.0)),
    )
    return picked.astype(jnp.bfloat16)


def add_rows(parts):
    return parts[0:1] + parts[1:2] + parts[2:3]


def mxu(left, right, left_dim, right_dim):
    return lax.dot_general(
        left, right, (((left_dim,), (right_dim,)), ((), ())), preferred_element_type=jnp.float32
    )


def row_times(row, matrix):
    return add_rows(mxu(split_rows(row), matrix, 1, 0))


def row_times_transposed(row, matrix):
    return add_rows(mxu(split_rows(row), matrix, 1, 1))


def place():
    feat = lax.axis_index("feat")
    samp = lax.axis_index("samp")
    return feat // QUAD, feat % QUAD, samp


def greet(peers):
    barrier = pltpu.get_barrier_semaphore()
    for peer in peers:
        pl.semaphore_signal(barrier, inc=1, device_id=peer, device_id_type=MESH)
    return lambda: pl.semaphore_wait(barrier, len(peers))


def remote(source, target, send_sem, recv_sem, peer):
    return pltpu.make_async_remote_copy(
        src_ref=source,
        dst_ref=target,
        send_sem=send_sem,
        recv_sem=recv_sem,
        device_id=peer,
        device_id_type=MESH,
    )


def start_exchange(slots, mine, peers, send_sems, recv_sems):
    copies = []
    for number, peer in enumerate(peers):
        copy = remote(
            slots.at[mine], slots.at[mine], send_sems.at[number], recv_sems.at[number], peer
        )
        copy.start()
        copies.append(copy)
    return copies


def finish(copies):
    for copy in copies:
        copy.wait()


def total_of(slots, count):
    value = slots[0]
    for number in range(1, count):
        value = value + slots[number]
    return value


def quad_peers(depth, quarter, samp):
    return [{"feat": depth * QUAD + (quarter + k) % QUAD, "samp": samp} for k in range(1, QUAD)]


def depth_peers(layers, depth, quarter, samp):
    return [
        {"feat": ((depth + k) % layers) * QUAD + quarter, "samp": samp} for k in range(1, layers)
    ]


def plane_peers(depth, quarter, samp):
    member = samp * QUAD + quarter
    peers = []
    for k in range(1, 2 * QUAD):
        other = (member + k) % (2 * QUAD)
        peers.append({"feat": depth * QUAD + other % QUAD, "samp": other // QUAD})
    return peers


CHUNKS = 4
AHEAD = 2


def gram_kernel(
    layers, features_home, weights, labels, sampled,
    scaled_home, gram_home, gradient, upper, lower, size,
    scaled, gram, inverse, pair, features, chosen, own_rows, sent_rows, came_rows, quad_slots, depth_slots, root_sent, root_came, grad_sent, grad_came,
    load_sem, store_sem, ship_send, ship_recv, quad_send, quad_recv, depth_send, depth_recv, small_send, small_recv,
):
    depth, quarter, samp = place()
    rows, columns = features.shape
    samples = sampled.shape[1]
    half = columns // 2
    partner = {"feat": depth * QUAD + quarter, "samp": 1 - samp}
    across = quad_peers(depth, quarter, samp)
    along = depth_peers(layers, depth, quarter, samp)
    mine_at = pl.multiple_of(samp * half, 128)
    other_at = pl.multiple_of((1 - samp) * half, 128)
    piece = samples // CHUNKS

    def load(number, start):
        return pltpu.make_async_copy(
            features_home.at[:, pl.ds(start, half)],
            features.at[:, pl.ds(start, half)],
            load_sem.at[number],
        )

    load_other, load_mine = load(0, other_at), load(1, mine_at)
    load_other.start()
    load_mine.start()
    wait_all = greet([partner] + across + along)

    def choose(first):
        wanted = jnp.transpose(jnp.broadcast_to(sampled[:, first : first + piece], (128, piece)))
        lane = lax.broadcasted_iota(jnp.int32, wanted.shape, 1)
        for start in range(0, rows, 128):
            hot = jnp.where(lane + start == wanted, 1.0, 0.0)
            chosen[first : first + piece, start : start + 128] = hot.astype(jnp.bfloat16)

    def ship(number):
        first = number * piece
        return remote(
            sent_rows.at[pl.ds(first, piece)],
            came_rows.at[pl.ds(first, piece)],
            ship_send.at[number],
            ship_recv.at[number],
            partner,
        )

    for number in range(CHUNKS):
        first = number * piece
        choose(first)
        if number == 0:
            load_other.wait()
        sent_rows[pl.ds(first, piece), :] = mxu(
            chosen[pl.ds(first, piece), :], features[:, pl.ds(other_at, half)], 1, 0
        ).astype(jnp.bfloat16)
        if number == 0:
            wait_all()
        if number < AHEAD:
            ship(number).start()
    load_mine.wait()
    quad_slots[quarter] = row_times_transposed(weights[...], features[...])
    quad_copies = start_exchange(quad_slots, quarter, across, quad_send, quad_recv)

    def pick_own(number, carry):
        first = pl.multiple_of(number * piece, 128)
        own_rows[pl.ds(first, piece), :] = mxu(
            chosen[pl.ds(first, piece), :], features[:, pl.ds(mine_at, half)], 1, 0
        ).astype(jnp.bfloat16)
        return carry

    finish(quad_copies)
    depth_slots[depth] = total_of(quad_slots, QUAD)
    depth_copies = start_exchange(depth_slots, depth, along, depth_send, depth_recv)
    lax.fori_loop(0, CHUNKS, pick_own, 0)
    finish(depth_copies)
    margin = total_of(depth_slots, layers)
    probability = 1.0 / (1.0 + jnp.exp(-margin))
    root = jnp.sqrt(probability * (1.0 - probability))
    own_root = row_times_transposed(root, chosen[...])
    root_sent[...] = own_root
    root_copy = remote(root_sent, root_came, small_send.at[0], small_recv.at[0], partner)
    root_copy.start()
    for number in range(AHEAD, CHUNKS):
        ship(number).start()
    residue = probability - labels[...].astype(jnp.float32)
    grad_sent[...] = row_times(residue, features[:, pl.ds(other_at, half)])
    grad_copy = remote(grad_sent, grad_came, small_send.at[1], small_recv.at[1], partner)
    grad_copy.start()
    own_grad = row_times(residue, features[:, pl.ds(mine_at, half)])

    def scale_into(source, factor, first, start):
        for column in range(0, half, 128):
            wide = source[pl.ds(first, piece), column : column + 128].astype(jnp.float32) * factor
            scaled[pl.ds(start, piece), column : column + 128] = wide.astype(jnp.bfloat16)

    def root_factor(root_row, number):
        part = root_row[:, number * piece : (number + 1) * piece]
        return jnp.transpose(jnp.broadcast_to(part, (128, piece)))

    mine_row = pl.multiple_of(samp * samples, 128)
    other_row = pl.multiple_of((1 - samp) * samples, 128)
    for number in range(CHUNKS):
        first = number * piece
        scale_into(own_rows, root_factor(own_root, number), first, mine_row + first)
    stores = [
        pltpu.make_async_copy(
            scaled.at[pl.ds(mine_row, samples)],
            scaled_home.at[pl.ds(mine_row, samples)],
            store_sem.at[CHUNKS],
        )
    ]
    stores[0].start()
    own_block = scaled[pl.ds(mine_row, samples), :]
    gram[...] = mxu(own_block, own_block, 0, 0)
    ridge_term = RIDGE_COEF / F
    shape = gram.shape
    same = lax.broadcasted_iota(jnp.int32, shape, 0) == lax.broadcasted_iota(jnp.int32, shape, 1)
    eye = jnp.where(same, 1.0, 0.0)
    bound = None
    for number in range(CHUNKS):
        first = number * piece
        if number == CHUNKS - 1:
            bound = early_inverse(gram[...] / (samples + first) + ridge_term * eye, eye, inverse, pair)
        ship(number).wait()
        if number == 0:
            root_copy.wait()
        scale_into(came_rows, root_factor(root_came[...], number), first, other_row + first)
        store = pltpu.make_async_copy(
            scaled.at[pl.ds(other_row + first, piece)],
            scaled_home.at[pl.ds(other_row + first, piece)],
            store_sem.at[number],
        )
        store.start()
        stores.append(store)
        block = scaled[pl.ds(other_row + first, piece), :]
        gram[...] += mxu(block, block, 0, 0)
    gram[...] = gram[...] / (2 * samples) + ridge_term * eye
    store = pltpu.make_async_copy(gram, gram_home, store_sem.at[CHUNKS + 1])
    store.start()
    stores.append(store)
    size[...] = jnp.broadcast_to(late_inverse(gram, bound, eye, inverse, pair, upper, lower), (1, 128))
    grad_copy.wait()
    gradient[...] = (own_grad + grad_came[...]) / (2 * rows) + ridge_term * weights[
        :, pl.ds(mine_at, half)
    ]
    for store in stores:
        store.wait()


SQUARINGS = 5
POLISH = 2
LIMIT = 60
DAMP = 0.6
SETTLED = 0.02


def halves(value):
    top = value.astype(jnp.bfloat16)
    return top, (value - top.astype(jnp.float32)).astype(jnp.bfloat16)


def raise_power(inverse, pair, count):
    order = inverse.shape[0]

    def square(_, carry):
        product = mxu(pair[...], pair[:order], 1, 0)
        value = inverse[...] + product[order:]
        inverse[...] = value
        pair[:order] = product[:order].astype(jnp.bfloat16)
        pair[order:] = value.astype(jnp.bfloat16)
        return carry

    lax.fori_loop(0, count - 1, square, 0)
    inverse[...] += mxu(pair[order:], pair[:order], 1, 0)


def early_inverse(early, eye, inverse, pair):
    order = early.shape[0]
    norm = lambda matrix: jnp.max(
        jnp.sum(jnp.abs(matrix), axis=0, keepdims=True), axis=1, keepdims=True
    )
    first_bound = norm(early)
    first = (early / first_bound).astype(jnp.bfloat16)
    squared = mxu(first, first, 1, 0)
    ratio = jnp.sqrt(norm(squared))
    bound = first_bound * ratio
    unit = early / bound
    value = 2.0 * eye - unit
    inverse[...] = value
    pair[:order] = (eye - 2.0 * unit + squared / (ratio * ratio)).astype(jnp.bfloat16)
    pair[order:] = value.astype(jnp.bfloat16)
    raise_power(inverse, pair, SQUARINGS)
    return bound


def late_inverse(gram, bound, eye, inverse, pair, upper, lower):
    order = gram.shape[0]
    unit_top, unit_low = halves(gram[...] / bound)
    value = DAMP * inverse[...]
    inverse[...] = value
    top = value.astype(jnp.bfloat16)
    pair[order:] = top
    pair[:order] = (eye - mxu(unit_top, top, 1, 0)).astype(jnp.bfloat16)
    raise_power(inverse, pair, 2)
    pair[:order] = unit_top
    pair[order:] = unit_low
    left = None
    for _ in range(POLISH):
        value = inverse[...]
        top, low = halves(value)
        product = mxu(pair[...], top, 1, 0)
        left = eye - (product[:order] + (product[order:] + mxu(pair[:order], low, 1, 0)))
        inverse[...] = value + mxu(top, left.astype(jnp.bfloat16), 1, 0)
    top, low = halves(inverse[...] / bound)
    upper[...] = top
    lower[...] = low
    return jnp.sum(jnp.sum(left * left, axis=0, keepdims=True), axis=1, keepdims=True)


def rescue_kernel(size, gram_home, _upper, _lower, upper_home, lower_home, unit, inverse, top_half, low_half):
    settled = size[0, 0] < SETTLED

    @pl.when(jnp.logical_not(settled))
    def _():
        pltpu.sync_copy(gram_home, unit)
        bound = jnp.max(jnp.sum(jnp.abs(unit[...]), axis=0, keepdims=True))
        unit[...] = unit[...] / bound
        shape = unit.shape
        eye = jnp.where(
            lax.broadcasted_iota(jnp.int32, shape, 0) == lax.broadcasted_iota(jnp.int32, shape, 1),
            1.0,
            0.0,
        )
        inverse[...] = eye

        def exact(left, right):
            return jnp.dot(
                left, right, precision=lax.Precision.HIGHEST, preferred_element_type=jnp.float32
            )

        def going(state):
            count, size_now = state
            return jnp.logical_and(count < LIMIT, size_now > 1e-8)

        def step(state):
            count, _ = state
            value = inverse[...]
            left = eye - exact(unit[...], value)
            fresh = value + exact(value, left)
            inverse[...] = 0.5 * (fresh + jnp.transpose(fresh))
            return count + 1, jnp.sum(left * left)

        lax.while_loop(going, step, (jnp.int32(0), jnp.float32(1.0)))
        top, low = halves(inverse[...] / bound)
        top_half[...] = top
        low_half[...] = low
        pltpu.sync_copy(top_half, upper_home)
        pltpu.sync_copy(low_half, lower_home)


def descent_kernel(
    layers, scaled_home, upper, lower, gradient,
    step,
    scaled, plane_slots, depth_slots, part_sent, part_came,
    load_sem, plane_send, plane_recv, depth_send, depth_recv, part_send, part_recv,
):
    depth, quarter, samp = place()
    samples, half = scaled.shape
    partner = {"feat": depth * QUAD + quarter, "samp": 1 - samp}
    plane = plane_peers(depth, quarter, samp)
    along = depth_peers(layers, depth, quarter, samp)
    load = pltpu.make_async_copy(scaled_home, scaled, load_sem.at[0])
    load.start()
    wait_all = greet(plane + along)
    member = samp * QUAD + quarter
    ridge_term = RIDGE_COEF / F
    lane = lax.broadcasted_iota(jnp.int32, (1, 128), 1)

    def precondition(vector):
        parts = split_rows(vector)
        return add_rows(mxu(parts, upper[...], 1, 0) + mxu(parts, lower[...], 1, 0))

    def total(row):
        return jnp.sum(row, axis=1, keepdims=True)

    residual = -gradient[...]
    answer = jnp.zeros_like(residual)
    direction = jnp.zeros_like(residual)
    twin_answer = jnp.zeros_like(residual)
    twin_direction = jnp.zeros_like(residual)
    along_rows = None
    rz_now = None
    length = None
    for iteration in range(ITERS):
        precond = precondition(residual)
        numbers = jnp.where(
            lane == 0,
            total(residual * precond),
            jnp.where(
                lane == 1,
                total(precond * precond),
                jnp.where(lane == 2, total(precond * direction), 0.0),
            ),
        )
        mine = plane_slots.at[iteration, member]
        part_sent[iteration] = precond
        if iteration == 0:
            load.wait()
        mine[:, :samples] = row_times_transposed(precond, scaled[...])
        mine[:, samples:] = numbers
        if iteration == 0:
            wait_all()
        plane_copies = start_exchange(
            plane_slots.at[iteration], member, plane, plane_send.at[iteration], plane_recv.at[iteration]
        )
        twin_copy = remote(
            part_sent.at[iteration],
            part_came.at[iteration],
            part_send.at[iteration],
            part_recv.at[iteration],
            partner,
        )
        twin_copy.start()
        finish(plane_copies)
        depth_slots[iteration, depth] = total_of(plane_slots.at[iteration], 2 * QUAD)
        finish(
            start_exchange(
                depth_slots.at[iteration], depth, along, depth_send.at[iteration], depth_recv.at[iteration]
            )
        )
        twin_copy.wait()
        twin_precond = part_came[iteration]
        summed = total_of(depth_slots.at[iteration], layers)
        image_rows = summed[:, :samples]
        fresh = summed[:, samples : samples + 1]
        square = summed[:, samples + 1 : samples + 2]
        cross = summed[:, samples + 2 : samples + 3]
        if iteration == 0:
            direction = precond
            twin_direction = twin_precond
            along_rows = image_rows
            length = square
        else:
            beta = fresh / rz_now
            direction = precond + beta * direction
            twin_direction = twin_precond + beta * twin_direction
            along_rows = image_rows + beta * along_rows
            length = square + 2.0 * beta * cross + beta * beta * length
        rz_now = fresh
        alpha = rz_now / (total(along_rows * along_rows) / samples + ridge_term * length)
        answer = answer + alpha * direction
        twin_answer = twin_answer + alpha * twin_direction
        if iteration + 1 < ITERS:
            image = row_times(along_rows, scaled[...]) / samples + ridge_term * direction
            residual = residual - alpha * image
    step[:, pl.ds(pl.multiple_of(samp * half, 128), half)] = answer
    step[:, pl.ds(pl.multiple_of((1 - samp) * half, 128), half)] = twin_answer


def split_device(features, labels, weights, sampled):
    rows, columns = features.shape
    samples = sampled.shape[0]
    half = columns // 2
    layers = lax.axis_size("feat") // QUAD
    shaped = jax.ShapeDtypeStruct
    whole = pl.BlockSpec(memory_space=pltpu.VMEM)
    dma = pltpu.SemaphoreType.DMA
    vmem = pltpu.VMEM
    anywhere = pl.BlockSpec(memory_space=pl.ANY)
    scaled, gram, gradient, upper, lower, size = pl.pallas_call(
        functools.partial(gram_kernel, layers),
        out_shape=(
            shaped((2 * samples, half), jnp.bfloat16),
            shaped((half, half), jnp.float32),
            shaped((1, half), jnp.float32),
            shaped((half, half), jnp.bfloat16),
            shaped((half, half), jnp.bfloat16),
            shaped((1, 128), jnp.float32),
        ),
        in_specs=[anywhere] + [whole] * 3,
        out_specs=(anywhere,) * 2 + (whole,) * 4,
        scratch_shapes=[
            vmem((2 * samples, half), jnp.bfloat16),
            vmem((half, half), jnp.float32),
            vmem((half, half), jnp.float32),
            vmem((2 * half, half), jnp.bfloat16),
            vmem((rows, columns), jnp.bfloat16),
            vmem((samples, rows), jnp.bfloat16),
            vmem((samples, half), jnp.bfloat16),
            vmem((samples, half), jnp.bfloat16),
            vmem((samples, half), jnp.bfloat16),
            vmem((QUAD, 1, rows), jnp.float32),
            vmem((layers, 1, rows), jnp.float32),
            vmem((1, samples), jnp.float32),
            vmem((1, samples), jnp.float32),
            vmem((1, half), jnp.float32),
            vmem((1, half), jnp.float32),
            dma((2,)),
            dma((CHUNKS + 2,)),
            dma((CHUNKS,)),
            dma((CHUNKS,)),
            dma((QUAD - 1,)),
            dma((QUAD - 1,)),
            dma((layers - 1,)),
            dma((layers - 1,)),
            dma((2,)),
            dma((2,)),
        ],
        compiler_params=pltpu.CompilerParams(collective_id=0, has_side_effects=True),
    )(features, weights[None, :], labels[None, :], sampled[None, :])
    upper, lower = pl.pallas_call(
        rescue_kernel,
        out_shape=(shaped((half, half), jnp.bfloat16),) * 2,
        in_specs=[pl.BlockSpec(memory_space=pltpu.SMEM)] + [anywhere] * 3,
        out_specs=(anywhere,) * 2,
        scratch_shapes=[
            vmem((half, half), jnp.float32),
            vmem((half, half), jnp.float32),
            vmem((half, half), jnp.bfloat16),
            vmem((half, half), jnp.bfloat16),
        ],
        input_output_aliases={2: 0, 3: 1},
    )(size, gram, upper, lower)
    width = 2 * samples + 128
    step = pl.pallas_call(
        functools.partial(descent_kernel, layers),
        out_shape=shaped((1, columns), jnp.float32),
        in_specs=[anywhere] + [whole] * 3,
        out_specs=whole,
        scratch_shapes=[
            vmem((2 * samples, half), jnp.bfloat16),
            vmem((ITERS, 2 * QUAD, 1, width), jnp.float32),
            vmem((ITERS, layers, 1, width), jnp.float32),
            vmem((ITERS, 1, half), jnp.float32),
            vmem((ITERS, 1, half), jnp.float32),
            dma((1,)),
            dma((ITERS, 2 * QUAD - 1)),
            dma((ITERS, 2 * QUAD - 1)),
            dma((ITERS, layers - 1)),
            dma((ITERS, layers - 1)),
            dma((ITERS,)),
            dma((ITERS,)),
        ],
        compiler_params=pltpu.CompilerParams(collective_id=1, has_side_effects=True),
    )(scaled, upper, lower, gradient)
    return step[0]


def solution(mesh):
    placed = (P("samp", "feat"), P("samp"), P("feat"), P("samp"))
    devices, groups = mesh.shape["feat"], mesh.shape["samp"]
    apart = groups == 2 and devices % QUAD == 0 and devices > QUAD and F // devices == 2 * BLK
    return jax.shard_map(
        split_device if apart else per_device,
        mesh=mesh,
        in_specs=placed,
        out_specs=P("feat"),
        check_vma=False,
    )
```
